256 devices in a mesh: tm: 64 (over z, y, core), series: 4 (over x).
Axes of the slice: x: 4, y: 4, z: 8, core: 2. Of those that a mesh axis runs over, the one named last changes fastest.
Arguments:
- series_values: bfloat16 [4096, 32768], P('tm', 'series'), may hold values from -4 to 4
- observed: int32 [4096, 32768], P('tm', 'series'), may hold values 0 or 1
- series_factors: bfloat16 [32768, 128], P('series'), may hold values from -0.03125 to 0.03125
- time_factors: float32 [4096, 128], P('tm'), may hold values from -6 to 6
- lag_weights: float32 [25, 128], replicated, may hold values from -0.5 to 0.5
Outputs:
- time_update: float32 [4096, 128], P('tm')
- misfit: bfloat16 [4096, 32768], P(None, ('series', 'tm'))
The draws below stay inside these ranges and needn't reach their ends.
Inputs may be any that keep to these rules, and one draw needn't show every extreme that they name: observed holds only 0 and 1.
All inputs are finite; a program needn't handle non-finite values. No bound on the sum of `observed` on one device may be relied on, other than what follows from the above.
Results may differ from the reference program's by a relative error of at most 0.005.
Values may be sent and summed in bfloat16 or wider, within the bound.
No kernel may reach another device: no remote copies, remote signals or barrier semaphores. Data moves between devices by JAX's collectives and lax.ppermute only.
A program may use at most 64 MiB of HBM per device.

```python
import jax
import jax.numpy as jnp
from jax import lax

K = 128
T_DEV = 64
SHORT = 24
SEASON = 168
ITERS = 3
NLAG = 25
NS = 32768
T_SIZE = 4096


def plant(entries, key, low, high):
    shape = entries.shape
    place = [jax.random.randint(jax.random.fold_in(key, axis), (), 0, shape[axis]) for axis in range(len(shape))]
    entries = entries.at[tuple(place)].set(low)
    longest = shape.index(max(shape))
    place[longest] = (place[longest] + 1) % shape[longest]
    return entries.at[tuple(place)].set(high)


def level_of(own_key, dims, cuts, smallest, largest):
    factor_of, own = 1.0, jax.random.fold_in(own_key, 6)
    for position, shards_of in cuts:
        steps = jnp.exp(jax.random.uniform(jax.random.fold_in(own, position), (shards_of,), jnp.float32, smallest / len(cuts), largest / len(cuts)))
        factor_of = factor_of * jnp.repeat(steps, dims[position] // shards_of).reshape([-1 if axis == position else 1 for axis in range(len(dims))])
    return factor_of


def bell_draw(key, dims, width, most, cuts=(), held_as=jnp.bfloat16):
    entries = width * jax.random.normal(key, dims, jnp.float32)
    if cuts:
        entries = entries * level_of(key, dims, cuts, -0.22, 0.18)
    return jnp.clip(entries, -most, most).astype(held_as)


def setup_inputs(seed: int = 0) -> dict:
    keys = jax.random.split(jax.random.key(seed), 6)
    return {
        "series_values": bell_draw(keys[0], (T_SIZE, NS), 1.0, 4.0, ((0, 64), (1, 4))),
        "observed": plant((jax.random.randint(keys[1], (T_SIZE, NS), 0, 2) < 1).astype(jnp.int32), jax.random.fold_in(keys[1], 1), 0, 1),
        "series_factors": bell_draw(keys[2], (NS, K), NS ** -0.5, 0.03125, ((0, 4),)),
        "time_factors": bell_draw(keys[3], (T_SIZE, K), 1.0, 6.0, ((0, 64),), jnp.float32),
        "lag_weights": jnp.clip(jax.random.uniform(keys[4], (NLAG, K), jnp.float32, -0.5, 0.5), -0.5, 0.5),
    }


data_weight = 2.0
penalty_weight = 0.5
ridge_weight = 0.2


def delays():
    return list(range(1, SHORT + 1)) + [SEASON]


def behind(current, lag_weights):
    time_rows, rank_width = current.shape
    result = current
    for number, lag_steps in enumerate(delays()):
        moved = jnp.concatenate([jnp.zeros((lag_steps, rank_width), jnp.float32), current[:time_rows - lag_steps]], axis=0)
        result = result - lag_weights[number] * moved
    return result


def ahead_of(current, lag_weights):
    time_rows, rank_width = current.shape
    result = current
    for number, lag_steps in enumerate(delays()):
        moved = jnp.concatenate([current[lag_steps:], jnp.zeros((lag_steps, rank_width), jnp.float32)], axis=0)
        result = result - lag_weights[number] * moved
    return result


def blocks(array):
    return array.reshape((array.shape[0] // T_DEV, T_DEV) + array.shape[1:])


def reference(series_values, observed, series_factors, time_factors, lag_weights):
    observed_blocks = blocks(observed == 1)
    value_blocks = blocks(series_values)

    def project_all(current):
        def one_block(pair):
            rows_here, mask_rows = pair
            fitted = jnp.dot(rows_here.astype(jnp.bfloat16), series_factors.T, preferred_element_type=jnp.float32)
            masked = jnp.where(mask_rows, fitted, 0.0).astype(jnp.bfloat16)
            return jnp.dot(masked, series_factors, preferred_element_type=jnp.float32)
        return lax.map(one_block, (blocks(current), observed_blocks)).reshape(current.shape)

    def operator(current):
        return data_weight * project_all(current) + penalty_weight * ahead_of(behind(current, lag_weights), lag_weights) + ridge_weight * current

    def target_block(pair):
        rows_here, mask_rows = pair
        kept = jnp.where(mask_rows, rows_here, jnp.zeros((), rows_here.dtype))
        return jnp.dot(kept, series_factors, preferred_element_type=jnp.float32)

    target = lax.map(target_block, (value_blocks, observed_blocks)).reshape(time_factors.shape)
    solution = time_factors
    residual = data_weight * target - operator(time_factors)
    direction = residual
    squared = jnp.sum(residual * residual)
    for step_number in range(ITERS):
        image = operator(direction)
        step_size = squared / jnp.sum(direction * image)
        solution = solution + step_size * direction
        residual = residual - step_size * image
        renewed = jnp.sum(residual * residual)
        direction = residual + (renewed / squared) * direction
        squared = renewed

    def misfit_block(pair):
        rows_here, factor_rows = pair
        fit_here = jnp.dot(factor_rows, series_factors.T, preferred_element_type=jnp.float32)
        return (rows_here.astype(jnp.float32) - fit_here).astype(jnp.bfloat16)

    final_low = solution.astype(jnp.bfloat16)
    misfit = lax.map(misfit_block, (value_blocks, blocks(final_low))).reshape(series_values.shape)
    return solution, misfit
```

```python
import jax
import jax.numpy as jnp
from jax import lax
from jax.sharding import PartitionSpec as P

SHORT = 24
SEASON = 168
LAGS = list(range(1, SHORT + 1)) + [SEASON]
data_weight = 2.0
penalty_weight = 0.5
ridge_weight = 0.2


def against(left_rows, factors):
    return lax.dot_general(
        left_rows, factors, (((1,), (1,)), ((), ())), preferred_element_type=jnp.float32
    )


def on_device(series_values, observed, series_factors, time_factors, lag_weights):
    rows, rank = time_factors.shape
    n_tm = lax.axis_size("tm")
    n_series = lax.axis_size("series")
    here = lax.axis_index("series")
    first_time = lax.axis_index("tm") * rows

    def route(steps):
        pairs = []
        for column, step in enumerate(steps):
            if step is None:
                continue
            for source in range(n_tm):
                target = source + step
                if 0 <= target < n_tm:
                    pairs.append((source * n_series + column, target * n_series + column))
        return pairs

    near_route = route([1, -1, 2, -2])
    far_route = route([3, -3, None, None])

    def fetch(field):
        near = jnp.where((here == 0) | (here == 3), field[16:64], field[0:48])
        far = jnp.where(here == 0, field[24:64], field[0:40])
        both = ("tm", "series")
        return lax.ppermute(near, both, near_route), lax.ppermute(far, both, far_route)

    def penalty_part(field, near, far):
        at = lambda column, part: jnp.where(here == column, part, 0.0)
        blank = lambda count: jnp.zeros((count, rank), jnp.float32)
        window = jnp.concatenate(
            [
                at(0, far),
                at(2, near),
                blank(32),
                at(0, near),
                at(2, field),
                at(1, near),
                blank(32),
                at(3, near),
                at(1, far),
            ],
            axis=0,
        )

        def lagged(start, count):
            result = window[SEASON + start : SEASON + start + count]
            for number, lag in enumerate(LAGS):
                begin = SEASON + start - lag
                result = result - lag_weights[number] * window[begin : begin + count]
            stamp = first_time + start + lax.broadcasted_iota(jnp.int32, (count, 1), 0)
            return jnp.where(stamp < n_tm * rows, result, 0.0)

        short = lagged(0, rows + SHORT)
        season = lagged(SEASON, rows)
        result = short[:rows]
        for number, lag in enumerate(LAGS[:-1]):
            result = result - lag_weights[number] * short[lag : lag + rows]
        return result - lag_weights[len(LAGS) - 1] * season

    def series_sum(part):
        def moved(distance):
            pairs = [(i, (i + distance) % n_series) for i in range(n_series)]
            return lax.ppermute(part, "series", pairs)

        return (part + moved(2)) + (moved(1) + moved(3))

    seen = observed == 1

    def fit(field):
        return jnp.where(seen, against(field.astype(jnp.bfloat16), series_factors), 0.0)

    def back(rows_here):
        return jnp.dot(rows_here, series_factors, preferred_element_type=jnp.float32)

    def image(field):
        near, far = fetch(field)
        local = back(fit(field).astype(jnp.bfloat16))
        part = data_weight * local + penalty_weight * penalty_part(field, near, far)
        return part

    kept = jnp.where(seen, series_values, jnp.zeros((), jnp.bfloat16))
    power0 = series_sum(data_weight * back(kept) - image(time_factors)) - ridge_weight * time_factors
    power1 = series_sum(image(power0)) + ridge_weight * power0
    power2 = series_sum(image(power1)) + ridge_weight * power1
    near, far = fetch(power2)
    fitted = fit(power2)
    share = 1.0 / n_series
    quadratic = data_weight * jnp.sum(fitted * fitted) + penalty_weight * jnp.sum(
        power2 * penalty_part(power2, near, far)
    )
    sums = [
        share * jnp.sum(power0 * power0),
        share * jnp.sum(power0 * power1),
        share * jnp.sum(power0 * power2),
        share * jnp.sum(power1 * power1),
        share * jnp.sum(power1 * power2),
        share * jnp.sum(power2 * power2),
        quadratic,
    ]
    lane = lax.broadcasted_iota(jnp.int32, (1, 128), 1)
    packed = jnp.zeros((1, 128), jnp.float32)
    for number, value in enumerate(sums):
        packed = jnp.where(lane == number, value, packed)
    everyone = n_tm * n_series
    spread = jnp.broadcast_to(packed[None], (everyone, 1, 128))
    gathered = lax.all_to_all(spread, ("tm", "series"), split_axis=0, concat_axis=0, tiled=True)
    total = jnp.sum(gathered, axis=(0, 1))
    m00, m01, m02, m11, m12, m22 = [total[number] for number in range(6)]
    m23 = total[6] + ridge_weight * m22

    alpha0 = m00 / m01
    norm1 = m00 - 2.0 * alpha0 * m01 + alpha0 * alpha0 * m11
    beta0 = norm1 / m00
    g0 = 1.0 + beta0
    curvature1 = g0 * g0 * m01 - g0 * alpha0 * (m02 + m11) + alpha0 * alpha0 * m12
    alpha1 = norm1 / curvature1
    a = -(alpha0 + alpha1 * g0)
    b = alpha0 * alpha1
    norm2 = m00 + a * a * m11 + b * b * m22 + 2.0 * (a * m01 + b * m02 + a * b * m12)
    beta1 = norm2 / norm1
    c = 1.0 + beta1 * g0
    d = a - beta1 * alpha0
    e = b
    curvature2 = (
        c * c * m01
        + c * d * (m02 + m11)
        + 2.0 * c * e * m12
        + d * d * m12
        + 2.0 * d * e * m22
        + e * e * m23
    )
    alpha2 = norm2 / curvature2
    k0 = alpha0 + alpha1 * g0 + alpha2 * c
    k1 = alpha2 * d - alpha1 * alpha0
    k2 = alpha2 * e
    solution_rows = time_factors + (k0 * power0 + k1 * power1 + k2 * power2)
    low = solution_rows.astype(jnp.bfloat16)
    local_misfit = (series_values.astype(jnp.float32) - against(low, series_factors)).astype(
        jnp.bfloat16
    )
    misfit = lax.all_to_all(local_misfit, "tm", split_axis=1, concat_axis=0, tiled=True)
    return solution_rows, misfit


def solution(mesh):
    placed = (P("tm", "series"), P("tm", "series"), P("series", None), P("tm", None), P())
    return jax.shard_map(
        on_device,
        mesh=mesh,
        in_specs=placed,
        out_specs=(P("tm", None), P(None, ("series", "tm"))),
        check_vma=False,
    )
```

```python
import functools

import jax
import jax.numpy as jnp
from jax import lax
from jax.experimental import pallas as pl
from jax.experimental.pallas import tpu as pltpu
from jax.sharding import PartitionSpec as P

SHORT = 24
SEASON = 168
LAGS = list(range(1, SHORT + 1)) + [SEASON]
NEAR = 48
FAR = 40
data_weight = 2.0
penalty_weight = 0.5
ridge_weight = 0.2

VMEM = pl.BlockSpec(memory_space=pltpu.VMEM)
SMEM = pl.BlockSpec(memory_space=pltpu.SMEM)
SMALL = pltpu.CompilerParams(vmem_limit_bytes=2 << 20)


def against(left_rows, factors):
    return lax.dot_general(
        left_rows, factors, (((1,), (1,)), ((), ())), preferred_element_type=jnp.float32
    )


def lag_product(place_ref, field, near, far, weights_ref, window, short, last_time):
    rows, rank = field.shape
    here = place_ref[0]
    first_time = place_ref[1]
    window[...] = jnp.zeros_like(window)
    window[SEASON : SEASON + rows, :] = jnp.where(here == 2, field, 0.0)
    near_at = jnp.where(
        here == 0, 120, jnp.where(here == 1, 232, jnp.where(here == 2, 40, 312))
    )
    far_at = jnp.where(here == 1, 360, 0)
    window[pl.ds(pl.multiple_of(near_at, 8), NEAR), :] = near
    window[pl.ds(pl.multiple_of(far_at, 8), FAR), :] = far

    def weight(number):
        return weights_ref[number : number + 1, :]

    def lagged(start, count):
        base = SEASON + start
        result = window[base : base + count, :]
        for number, lag in enumerate(LAGS):
            result = result - weight(number) * window[base - lag : base - lag + count, :]
        stamp = first_time + start + lax.broadcasted_iota(jnp.int32, (count, rank), 0)
        return jnp.where(stamp < last_time, result, 0.0)

    short[...] = lagged(0, rows + SHORT)
    result = short[0:rows, :] - weight(SHORT) * lagged(SEASON, rows)
    for number in range(SHORT):
        lag = LAGS[number]
        result = result - weight(number) * short[lag : lag + rows, :]
    return result


def penalty_kernel(
    scale, last_time, place_ref, field_ref, near_ref, far_ref, weights_ref, local_ref,
    part_ref, window, short,
):
    product = lag_product(
        place_ref, field_ref[...], near_ref[...], far_ref[...], weights_ref, window, short, last_time
    )
    part_ref[...] = data_weight * local_ref[...] + scale * product


def sum_kernel(
    scale, place_ref, own_ref, first_ref, second_ref, third_ref, field_ref,
    total_ref, low_ref, near_ref, far_ref,
):
    here = place_ref[0]
    total = (own_ref[...] + second_ref[...]) + (first_ref[...] + third_ref[...])
    total = total + scale * field_ref[...]
    total_ref[...] = total
    low_ref[...] = total.astype(jnp.bfloat16)
    rows = total.shape[0]
    late = jnp.logical_or(here == 0, here == 3)
    near_ref[...] = jnp.where(late, total[rows - NEAR :], total[:NEAR])
    far_ref[...] = jnp.where(here == 0, total[rows - FAR :], total[:FAR])


def moments_kernel(
    share, last_time, place_ref, squares_ref, zero_ref, one_ref, two_ref, near_ref, far_ref,
    weights_ref, spread_ref, window, short,
):
    zero, one, two = zero_ref[...], one_ref[...], two_ref[...]
    product = lag_product(
        place_ref, two, near_ref[...], far_ref[...], weights_ref, window, short, last_time
    )

    def inner(left, right):
        return jnp.sum(jnp.sum(left * right, axis=0, keepdims=True), axis=1, keepdims=True)

    sums = [
        share * inner(zero, zero),
        share * inner(zero, one),
        share * inner(zero, two),
        share * inner(one, one),
        share * inner(one, two),
        share * inner(two, two),
        data_weight * squares_ref[0, 0] + penalty_weight * inner(two, product),
    ]
    lane = lax.broadcasted_iota(jnp.int32, (1, zero.shape[1]), 1)
    packed = jnp.zeros((1, zero.shape[1]), jnp.float32)
    for number, value in enumerate(sums):
        packed = jnp.where(lane == number, value, packed)
    spread_ref[...] = jnp.broadcast_to(packed[None], spread_ref.shape)


def update_kernel(gathered_ref, start_ref, zero_ref, one_ref, two_ref, final_ref, low_ref):
    total = jnp.sum(gathered_ref[...], axis=0)
    lane = lax.broadcasted_iota(jnp.int32, total.shape, 1)

    def pick(number):
        return jnp.sum(jnp.where(lane == number, total, 0.0), axis=1, keepdims=True)

    m00, m01, m02, m11, m12, m22, m23 = [pick(number) for number in range(7)]
    m23 = m23 + ridge_weight * m22
    alpha0 = m00 / m01
    norm1 = m00 - 2.0 * alpha0 * m01 + alpha0 * alpha0 * m11
    g0 = 1.0 + norm1 / m00
    curvature1 = g0 * g0 * m01 - g0 * alpha0 * (m02 + m11) + alpha0 * alpha0 * m12
    alpha1 = norm1 / curvature1
    a = -(alpha0 + alpha1 * g0)
    b = alpha0 * alpha1
    norm2 = m00 + a * a * m11 + b * b * m22 + 2.0 * (a * m01 + b * m02 + a * b * m12)
    beta1 = norm2 / norm1
    c = 1.0 + beta1 * g0
    d = a - beta1 * alpha0
    curvature2 = (
        c * c * m01
        + c * d * (m02 + m11)
        + 2.0 * c * b * m12
        + d * d * m12
        + 2.0 * d * b * m22
        + b * b * m23
    )
    alpha2 = norm2 / curvature2
    k0 = alpha0 + alpha1 * g0 + alpha2 * c
    k1 = alpha2 * d - alpha1 * alpha0
    k2 = alpha2 * b
    final = start_ref[...] + (k0 * zero_ref[...] + k1 * one_ref[...] + k2 * two_ref[...])
    final_ref[...] = final
    low_ref[...] = final.astype(jnp.bfloat16)


def on_device(series_values, observed, series_factors, time_factors, lag_weights):
    rows, rank = time_factors.shape
    n_tm = lax.axis_size("tm")
    n_series = lax.axis_size("series")
    everyone = n_tm * n_series
    last_time = n_tm * rows
    here = lax.axis_index("series")
    place = jnp.stack([here, lax.axis_index("tm") * rows]).astype(jnp.int32)
    field_shape = jax.ShapeDtypeStruct((rows, rank), jnp.float32)
    low_shape = jax.ShapeDtypeStruct((rows, rank), jnp.bfloat16)
    lag_scratch = [
        pltpu.VMEM((2 * SEASON + rows, rank), jnp.float32),
        pltpu.VMEM((rows + SHORT, rank), jnp.float32),
    ]

    def route(steps):
        pairs = []
        for column, step in enumerate(steps):
            if step is None:
                continue
            for source in range(n_tm):
                target = source + step
                if 0 <= target < n_tm:
                    pairs.append((source * n_series + column, target * n_series + column))
        return pairs

    near_route = route([1, -1, 2, -2])
    far_route = route([3, -3, None, None])

    def fetch(near, far):
        both = ("tm", "series")
        return lax.ppermute(near, both, near_route), lax.ppermute(far, both, far_route)

    def penalty(scale, field, near, far, local):
        return pl.pallas_call(
            functools.partial(penalty_kernel, scale, last_time),
            out_shape=field_shape,
            in_specs=[SMEM] + [VMEM] * 5,
            out_specs=VMEM,
            scratch_shapes=lag_scratch,
            compiler_params=SMALL,
        )(place, field, near, far, lag_weights, local)

    def series_sum(scale, part, field):
        def moved(distance):
            pairs = [(i, (i + distance) % n_series) for i in range(n_series)]
            return lax.ppermute(part, "series", pairs)

        return pl.pallas_call(
            functools.partial(sum_kernel, scale),
            out_shape=(
                field_shape,
                low_shape,
                jax.ShapeDtypeStruct((NEAR, rank), jnp.float32),
                jax.ShapeDtypeStruct((FAR, rank), jnp.float32),
            ),
            in_specs=[SMEM] + [VMEM] * 5,
            out_specs=(VMEM,) * 4,
            compiler_params=SMALL,
        )(place, part, moved(1), moved(2), moved(3), field)

    seen = observed == 1

    def fit(low):
        return jnp.where(seen, against(low, series_factors), 0.0)

    def back(rows_here):
        return jnp.dot(rows_here, series_factors, preferred_element_type=jnp.float32)

    late = (here == 0) | (here == 3)
    near = jnp.where(late, time_factors[rows - NEAR :], time_factors[:NEAR])
    far = jnp.where(here == 0, time_factors[rows - FAR :], time_factors[:FAR])
    near, far = fetch(near, far)
    kept = jnp.where(seen, series_values, jnp.zeros((), jnp.bfloat16))
    local = back(kept) - back(fit(time_factors.astype(jnp.bfloat16)).astype(jnp.bfloat16))
    part = penalty(-penalty_weight, time_factors, near, far, local)
    power0, low, near, far = series_sum(-ridge_weight, part, time_factors)

    def image(field, low, near, far):
        near, far = fetch(near, far)
        local = back(fit(low).astype(jnp.bfloat16))
        part = penalty(penalty_weight, field, near, far, local)
        return series_sum(ridge_weight, part, field)

    power1, low, near, far = image(power0, low, near, far)
    power2, low, near, far = image(power1, low, near, far)
    near, far = fetch(near, far)
    fitted = fit(low)
    squares = jnp.sum(fitted * fitted).reshape(1, 1)
    spread = pl.pallas_call(
        functools.partial(moments_kernel, 1.0 / n_series, last_time),
        out_shape=jax.ShapeDtypeStruct((everyone, 1, rank), jnp.float32),
        in_specs=[SMEM, SMEM] + [VMEM] * 6,
        out_specs=VMEM,
        scratch_shapes=lag_scratch,
        compiler_params=SMALL,
    )(place, squares, power0, power1, power2, near, far, lag_weights)
    gathered = lax.all_to_all(spread, ("tm", "series"), split_axis=0, concat_axis=0, tiled=True)
    final, final_low = pl.pallas_call(
        update_kernel,
        out_shape=(field_shape, low_shape),
        in_specs=[VMEM] * 5,
        out_specs=(VMEM, VMEM),
        compiler_params=SMALL,
    )(gathered, time_factors, power0, power1, power2)
    local_misfit = (series_values.astype(jnp.float32) - against(final_low, series_factors)).astype(
        jnp.bfloat16
    )
    misfit = lax.all_to_all(local_misfit, "tm", split_axis=1, concat_axis=0, tiled=True)
    return final, misfit


def solution(mesh):
    placed = (P("tm", "series"), P("tm", "series"), P("series", None), P("tm", None), P())
    return jax.shard_map(
        on_device,
        mesh=mesh,
        in_specs=placed,
        out_specs=(P("tm", None), P(None, ("series", "tm"))),
        check_vma=False,
    )
```

```python
import functools

import jax
import jax.numpy as jnp
from jax import lax
from jax.experimental import pallas as pl
from jax.experimental.pallas import tpu as pltpu
from jax.sharding import PartitionSpec as P

SHORT = 24
SEASON = 168
LAGS = list(range(1, SHORT + 1)) + [SEASON]
MANY = 48
FEW = 24
EDGE = SEASON + 8
data_weight = 2.0
penalty_weight = 0.5
ridge_weight = 0.2

VMEM = pl.BlockSpec(memory_space=pltpu.VMEM)
SMEM = pl.BlockSpec(memory_space=pltpu.SMEM)
SMALL = pltpu.CompilerParams(vmem_limit_bytes=2 << 20)


def against(left_rows, factors):
    return lax.dot_general(
        left_rows, factors, (((1,), (1,)), ((), ())), preferred_element_type=jnp.float32
    )


def lag_product(place_ref, blocks, weights_ref, window, short, last_time):
    rank = weights_ref.shape[1]
    rows = window.shape[0] - 2 * EDGE
    first_time = place_ref[1]
    window[...] = jnp.zeros_like(window)
    for start, block in blocks:
        if not isinstance(start, int):
            start = pl.multiple_of(start, 8)
        window[pl.ds(start, block.shape[0]), :] = block

    def weight(number):
        return weights_ref[number : number + 1, :]

    def lagged(start, count):
        base = EDGE + start
        result = window[base : base + count, :]
        for number, lag in enumerate(LAGS):
            result = result - weight(number) * window[base - lag : base - lag + count, :]
        stamp = first_time + start + lax.broadcasted_iota(jnp.int32, (count, rank), 0)
        return jnp.where(stamp < last_time, result, 0.0)

    short[...] = lagged(0, rows + SHORT)
    result = short[0:rows, :] - weight(SHORT) * lagged(SEASON, rows)
    for number in range(SHORT):
        lag = LAGS[number]
        result = result - weight(number) * short[lag : lag + rows, :]
    return result


def penalty_kernel(
    scale, last_time, place_ref, field_ref, many_ref, few_ref, weights_ref, local_ref,
    part_ref, window, short,
):
    here = place_ref[0]
    many_at = jnp.where(
        here == 0, 0, jnp.where(here == 1, 368, jnp.where(here == 2, 48, 320))
    )
    blocks = [
        (EDGE, jnp.where(here == 0, field_ref[...], 0.0)),
        (many_at, many_ref[...]),
        (jnp.where(here == 3, 240, 152), few_ref[...]),
    ]
    product = lag_product(place_ref, blocks, weights_ref, window, short, last_time)
    part_ref[...] = data_weight * local_ref[...] + scale * product


def halo(here, field, many_ref, few_ref):
    rows = field.shape[0]
    late = jnp.logical_or(here == 0, here == 3)
    many_ref[...] = jnp.where(late, field[rows - MANY :], field[:MANY])
    few_ref[...] = jnp.where(here == 2, field[rows - FEW :], field[:FEW])


def start_kernel(place_ref, field_ref, low_ref, many_ref, few_ref):
    field = field_ref[...]
    low_ref[...] = field.astype(jnp.bfloat16)
    halo(place_ref[0], field, many_ref, few_ref)


def sum_kernel(
    scale, place_ref, own_ref, first_ref, second_ref, third_ref, field_ref,
    total_ref, low_ref, many_ref, few_ref,
):
    here = place_ref[0]
    total = (own_ref[...] + second_ref[...]) + (first_ref[...] + third_ref[...])
    total = total + scale * field_ref[...]
    total_ref[...] = total
    low_ref[...] = total.astype(jnp.bfloat16)
    halo(here, total, many_ref, few_ref)


def moments_kernel(
    share, last_time, place_ref, squares_ref, zero_ref, one_ref, two_ref, many_ref,
    weights_ref, spread_ref, window, short,
):
    zero, one, two = zero_ref[...], one_ref[...], two_ref[...]
    here = place_ref[0]
    many_at = jnp.where(here == 0, 0, jnp.where(here == 2, 48, 128))
    blocks = [
        (EDGE, jnp.where(here == 1, two, 0.0)),
        (many_at, jnp.where(here == 1, 0.0, 2.0 * many_ref[...])),
    ]
    product = lag_product(place_ref, blocks, weights_ref, window, short, last_time)

    def inner(left, right):
        return jnp.sum(jnp.sum(left * right, axis=0, keepdims=True), axis=1, keepdims=True)

    sums = [
        share * inner(zero, zero),
        share * inner(zero, one),
        share * inner(zero, two),
        share * inner(one, one),
        share * inner(one, two),
        share * inner(two, two),
        data_weight * squares_ref[0, 0] + penalty_weight * inner(two, product),
    ]
    lane = lax.broadcasted_iota(jnp.int32, (1, zero.shape[1]), 1)
    packed = jnp.zeros((1, zero.shape[1]), jnp.float32)
    for number, value in enumerate(sums):
        packed = jnp.where(lane == number, value, packed)
    spread_ref[...] = jnp.broadcast_to(packed[None], spread_ref.shape)


def update_kernel(
    gathered_ref, start_ref, zero_ref, one_ref, two_ref, values_ref, factors_ref,
    final_ref, misfit_ref,
):
    total = jnp.sum(gathered_ref[...], axis=0)
    lane = lax.broadcasted_iota(jnp.int32, total.shape, 1)

    def pick(number):
        return jnp.sum(jnp.where(lane == number, total, 0.0), axis=1, keepdims=True)

    m00, m01, m02, m11, m12, m22, m23 = [pick(number) for number in range(7)]
    m23 = m23 + ridge_weight * m22
    alpha0 = m00 / m01
    norm1 = m00 - 2.0 * alpha0 * m01 + alpha0 * alpha0 * m11
    g0 = 1.0 + norm1 / m00
    curvature1 = g0 * g0 * m01 - g0 * alpha0 * (m02 + m11) + alpha0 * alpha0 * m12
    alpha1 = norm1 / curvature1
    a = -(alpha0 + alpha1 * g0)
    b = alpha0 * alpha1
    norm2 = m00 + a * a * m11 + b * b * m22 + 2.0 * (a * m01 + b * m02 + a * b * m12)
    beta1 = norm2 / norm1
    c = 1.0 + beta1 * g0
    d = a - beta1 * alpha0
    curvature2 = (
        c * c * m01
        + c * d * (m02 + m11)
        + 2.0 * c * b * m12
        + d * d * m12
        + 2.0 * d * b * m22
        + b * b * m23
    )
    alpha2 = norm2 / curvature2
    k0 = alpha0 + alpha1 * g0 + alpha2 * c
    k1 = alpha2 * d - alpha1 * alpha0
    k2 = alpha2 * b
    final = start_ref[...] + (k0 * zero_ref[...] + k1 * one_ref[...] + k2 * two_ref[...])
    final_ref[...] = final
    low = final.astype(jnp.bfloat16)
    lanes = misfit_ref.shape[2]
    for first in range(0, values_ref.shape[1], 2 * lanes):
        columns = slice(first, first + 2 * lanes)
        fitted = against(low, factors_ref[columns, :])
        block = (values_ref[:, columns].astype(jnp.float32) - fitted).astype(jnp.bfloat16)
        misfit_ref[first // lanes] = block[:, :lanes]
        misfit_ref[first // lanes + 1] = block[:, lanes:]


def on_device(series_values, observed, series_factors, time_factors, lag_weights):
    rows, rank = time_factors.shape
    n_tm = lax.axis_size("tm")
    n_series = lax.axis_size("series")
    everyone = n_tm * n_series
    last_time = n_tm * rows
    here = lax.axis_index("series")
    place = jnp.stack([here, lax.axis_index("tm") * rows]).astype(jnp.int32)
    field_shape = jax.ShapeDtypeStruct((rows, rank), jnp.float32)
    many_shape = jax.ShapeDtypeStruct((MANY, rank), jnp.float32)
    few_shape = jax.ShapeDtypeStruct((FEW, rank), jnp.float32)
    low_shape = jax.ShapeDtypeStruct((rows, rank), jnp.bfloat16)
    lag_scratch = [
        pltpu.VMEM((2 * EDGE + rows, rank), jnp.float32),
        pltpu.VMEM((rows + SHORT, rank), jnp.float32),
    ]

    def route(steps):
        pairs = []
        for column, step in enumerate(steps):
            if step is None:
                continue
            for source in range(n_tm):
                target = source + step
                if 0 <= target < n_tm:
                    pairs.append((source * n_series + column, target * n_series + column))
        return pairs

    many_route = route([3, -3, 2, -2])
    few_route = route([None, None, 1, -1])
    last_route = route([3, None, 2, 1])
    both = ("tm", "series")

    def fetch(many, few):
        few = lax.ppermute(few, both, few_route)
        return lax.ppermute(many, both, many_route), few

    def penalty(scale, field, many, few, local):
        return pl.pallas_call(
            functools.partial(penalty_kernel, scale, last_time),
            out_shape=field_shape,
            in_specs=[SMEM] + [VMEM] * 5,
            out_specs=VMEM,
            scratch_shapes=lag_scratch,
            compiler_params=SMALL,
        )(place, field, many, few, lag_weights, local)

    def series_sum(scale, part, field):
        def moved(distance):
            pairs = [(i, (i + distance) % n_series) for i in range(n_series)]
            return lax.ppermute(part, "series", pairs)

        first, third = moved(1), moved(3)
        second = moved(2)
        return pl.pallas_call(
            functools.partial(sum_kernel, scale),
            out_shape=(
                field_shape,
                low_shape,
                many_shape,
                few_shape,
            ),
            in_specs=[SMEM] + [VMEM] * 5,
            out_specs=(VMEM,) * 4,
            compiler_params=SMALL,
        )(place, part, first, second, third, field)

    seen = observed == 1

    def fit(low):
        return jnp.where(seen, against(low, series_factors), 0.0)

    def back(rows_here):
        return jnp.dot(rows_here, series_factors, preferred_element_type=jnp.float32)

    low, many, few = pl.pallas_call(
        start_kernel,
        out_shape=(low_shape, many_shape, few_shape),
        in_specs=[SMEM, VMEM],
        out_specs=(VMEM,) * 3,
        compiler_params=SMALL,
    )(place, time_factors)
    many, few = fetch(many, few)
    kept = jnp.where(seen, series_values, jnp.zeros((), jnp.bfloat16))
    local = back(kept) - back(fit(low).astype(jnp.bfloat16))
    part = penalty(-penalty_weight, time_factors, many, few, local)
    power0, low, many, few = series_sum(-ridge_weight, part, time_factors)

    def image(field, low, many, few):
        many, few = fetch(many, few)
        local = back(fit(low).astype(jnp.bfloat16))
        part = penalty(penalty_weight, field, many, few, local)
        return series_sum(ridge_weight, part, field)

    power1, low, many, few = image(power0, low, many, few)
    power2, low, many, few = image(power1, low, many, few)
    many = lax.ppermute(many, both, last_route)
    fitted = fit(low)
    squares = jnp.sum(fitted * fitted).reshape(1, 1)
    spread = pl.pallas_call(
        functools.partial(moments_kernel, 1.0 / n_series, last_time),
        out_shape=jax.ShapeDtypeStruct((everyone, 1, rank), jnp.float32),
        in_specs=[SMEM, SMEM] + [VMEM] * 5,
        out_specs=VMEM,
        scratch_shapes=lag_scratch,
        compiler_params=SMALL,
    )(place, squares, power0, power1, power2, many, lag_weights)
    gathered = lax.all_to_all(spread, both, split_axis=0, concat_axis=0, tiled=True)
    final, misfit = pl.pallas_call(
        update_kernel,
        out_shape=(field_shape, jax.ShapeDtypeStruct((n_tm, rows, rank), jnp.bfloat16)),
        in_specs=[VMEM] * 7,
        out_specs=(VMEM, VMEM),
        compiler_params=SMALL,
    )(gathered, time_factors, power0, power1, power2, series_values, series_factors)
    misfit = lax.all_to_all(misfit, "tm", split_axis=0, concat_axis=0, tiled=True)
    return final, misfit.reshape(n_tm * rows, rank)


def solution(mesh):
    placed = (P("tm", "series"), P("tm", "series"), P("series", None), P("tm", None), P())
    return jax.shard_map(
        on_device,
        mesh=mesh,
        in_specs=placed,
        out_specs=(P("tm", None), P(None, ("series", "tm"))),
        check_vma=False,
    )
```

```python
import functools

import jax
import jax.numpy as jnp
from jax import lax
from jax.experimental import pallas as pl
from jax.experimental.pallas import tpu as pltpu
from jax.sharding import PartitionSpec as P

SHORT = 24
SEASON = 168
LAGS = list(range(1, SHORT + 1)) + [SEASON]
MANY = 48
REACH = (24, 48, 40)
EDGE = SEASON + 8
data_weight = 2.0
penalty_weight = 0.5
ridge_weight = 0.2

VMEM = pl.BlockSpec(memory_space=pltpu.VMEM)
SMEM = pl.BlockSpec(memory_space=pltpu.SMEM)
SMALL = pltpu.CompilerParams(vmem_limit_bytes=2 << 20)


def against(left_rows, factors):
    return lax.dot_general(
        left_rows, factors, (((1,), (1,)), ((), ())), preferred_element_type=jnp.float32
    )


def lag_product(place_ref, blocks, weights_ref, window, short, last_time):
    rank = weights_ref.shape[1]
    rows = window.shape[0] - 2 * EDGE
    first_time = place_ref[1]
    window[...] = jnp.zeros_like(window)
    for start, block in blocks:
        if not isinstance(start, int):
            start = pl.multiple_of(start, 8)
        window[pl.ds(start, block.shape[0]), :] = block

    def weight(number):
        return weights_ref[number : number + 1, :]

    def lagged(start, count):
        base = EDGE + start
        result = window[base : base + count, :]
        for number, lag in enumerate(LAGS):
            result = result - weight(number) * window[base - lag : base - lag + count, :]
        stamp = first_time + start + lax.broadcasted_iota(jnp.int32, (count, rank), 0)
        return jnp.where(stamp < last_time, result, 0.0)

    short[...] = lagged(0, rows + SHORT)
    result = short[0:rows, :] - weight(SHORT) * lagged(SEASON, rows)
    for number in range(SHORT):
        lag = LAGS[number]
        result = result - weight(number) * short[lag : lag + rows, :]
    return result


def penalty_kernel(
    scale, last_time, place_ref, field_ref, one_ref, two_ref, three_ref, weights_ref, local_ref,
    other_ref, part_ref, window, short,
):
    behind = place_ref[0] < 2
    blocks = [
        (EDGE, jnp.where(behind, field_ref[...], 0.0)),
        (jnp.where(behind, 152, 240), one_ref[...]),
        (jnp.where(behind, 48, 320), two_ref[...]),
        (jnp.where(behind, 8, 368), three_ref[...]),
    ]
    product = lag_product(place_ref, blocks, weights_ref, window, short, last_time)
    part_ref[...] = data_weight * (local_ref[...] + other_ref[...]) + scale * product


def halo(here, field, one_ref, two_ref, three_ref):
    rows = field.shape[0]
    behind = here < 2
    one_ref[...] = jnp.where(behind, field[rows - REACH[0] :], field[: REACH[0]])
    two_ref[...] = jnp.where(behind, field[: REACH[1]], field[rows - REACH[1] :])
    three_ref[...] = jnp.where(behind, field[rows - REACH[2] :], field[: REACH[2]])


def start_kernel(place_ref, field_ref, low_ref, one_ref, two_ref, three_ref):
    field = field_ref[...]
    low_ref[...] = field.astype(jnp.bfloat16)
    halo(place_ref[0], field, one_ref, two_ref, three_ref)


def sum_kernel(scale, place_ref, own_ref, other_ref, field_ref, total_ref, low_ref, *halo_refs):
    here = place_ref[0]
    total = (own_ref[...] + other_ref[...]) + scale * field_ref[...]
    total_ref[...] = total
    low_ref[...] = total.astype(jnp.bfloat16)
    if len(halo_refs) == 1:
        rows = total.shape[0]
        halo_refs[0][...] = jnp.where(here == 2, total[:MANY], total[rows - MANY :])
    else:
        halo(here, total, *halo_refs)


def moments_kernel(
    share, last_time, place_ref, squares_ref, zero_ref, one_ref, two_ref, many_ref,
    weights_ref, spread_ref, window, short,
):
    zero, one, two = zero_ref[...], one_ref[...], two_ref[...]
    here = place_ref[0]
    many_at = jnp.where(here == 0, 0, jnp.where(here == 2, 48, 128))
    blocks = [
        (EDGE, jnp.where(here == 1, two, 0.0)),
        (many_at, jnp.where(here == 1, 0.0, 2.0 * many_ref[...])),
    ]
    product = lag_product(place_ref, blocks, weights_ref, window, short, last_time)

    def inner(left, right):
        return jnp.sum(jnp.sum(left * right, axis=0, keepdims=True), axis=1, keepdims=True)

    sums = [
        share * inner(zero, zero),
        share * inner(zero, one),
        share * inner(zero, two),
        share * inner(one, one),
        share * inner(one, two),
        share * inner(two, two),
        data_weight * squares_ref[0, 0] + penalty_weight * inner(two, product),
    ]
    lane = lax.broadcasted_iota(jnp.int32, (1, zero.shape[1]), 1)
    packed = jnp.zeros((1, zero.shape[1]), jnp.float32)
    for number, value in enumerate(sums):
        packed = jnp.where(lane == number, value, packed)
    spread_ref[...] = jnp.broadcast_to(packed[None], spread_ref.shape)


def update_kernel(
    gathered_ref, start_ref, zero_ref, one_ref, two_ref, values_ref, factors_ref,
    final_ref, misfit_ref,
):
    total = jnp.sum(gathered_ref[...], axis=0)
    lane = lax.broadcasted_iota(jnp.int32, total.shape, 1)

    def pick(number):
        return jnp.sum(jnp.where(lane == number, total, 0.0), axis=1, keepdims=True)

    m00, m01, m02, m11, m12, m22, m23 = [pick(number) for number in range(7)]
    m23 = m23 + ridge_weight * m22
    alpha0 = m00 / m01
    norm1 = m00 - 2.0 * alpha0 * m01 + alpha0 * alpha0 * m11
    g0 = 1.0 + norm1 / m00
    curvature1 = g0 * g0 * m01 - g0 * alpha0 * (m02 + m11) + alpha0 * alpha0 * m12
    alpha1 = norm1 / curvature1
    a = -(alpha0 + alpha1 * g0)
    b = alpha0 * alpha1
    norm2 = m00 + a * a * m11 + b * b * m22 + 2.0 * (a * m01 + b * m02 + a * b * m12)
    beta1 = norm2 / norm1
    c = 1.0 + beta1 * g0
    d = a - beta1 * alpha0
    curvature2 = (
        c * c * m01
        + c * d * (m02 + m11)
        + 2.0 * c * b * m12
        + d * d * m12
        + 2.0 * d * b * m22
        + b * b * m23
    )
    alpha2 = norm2 / curvature2
    k0 = alpha0 + alpha1 * g0 + alpha2 * c
    k1 = alpha2 * d - alpha1 * alpha0
    k2 = alpha2 * b
    final = start_ref[...] + (k0 * zero_ref[...] + k1 * one_ref[...] + k2 * two_ref[...])
    final_ref[...] = final
    low = final.astype(jnp.bfloat16)
    lanes = misfit_ref.shape[2]
    for first in range(0, values_ref.shape[1], 2 * lanes):
        columns = slice(first, first + 2 * lanes)
        fitted = against(low, factors_ref[columns, :])
        block = (values_ref[:, columns].astype(jnp.float32) - fitted).astype(jnp.bfloat16)
        misfit_ref[first // lanes] = block[:, :lanes]
        misfit_ref[first // lanes + 1] = block[:, lanes:]


def on_device(series_values, observed, series_factors, time_factors, lag_weights):
    rows, rank = time_factors.shape
    n_tm = lax.axis_size("tm")
    n_series = lax.axis_size("series")
    everyone = n_tm * n_series
    last_time = n_tm * rows
    here = lax.axis_index("series")
    place = jnp.stack([here, lax.axis_index("tm") * rows]).astype(jnp.int32)
    field_shape = jax.ShapeDtypeStruct((rows, rank), jnp.float32)
    halo_shapes = tuple(jax.ShapeDtypeStruct((count, rank), jnp.float32) for count in REACH)
    last_shape = (jax.ShapeDtypeStruct((MANY, rank), jnp.float32),)
    low_shape = jax.ShapeDtypeStruct((rows, rank), jnp.bfloat16)
    lag_scratch = [
        pltpu.VMEM((2 * EDGE + rows, rank), jnp.float32),
        pltpu.VMEM((rows + SHORT, rank), jnp.float32),
    ]

    def route(steps):
        pairs = []
        for column, step in enumerate(steps):
            if step is None:
                continue
            for source in range(n_tm):
                target = source + step
                if 0 <= target < n_tm:
                    pairs.append((source * n_series + column, target * n_series + column))
        return pairs

    routes = [route([step, step, -step, -step]) for step in (1, 2, 3)]
    last_route = route([3, None, 2, 1])
    both = ("tm", "series")

    def with_pair(field, partner):
        return lax.ppermute(field, "series", [(i, partner(i)) for i in range(n_series)])

    def finish(scale, field, halos, local, ridge, out_halos):
        fetched = [lax.ppermute(rows_out, both, pairs) for rows_out, pairs in zip(halos, routes)]
        other = with_pair(local, lambda i: i ^ 1)
        part = pl.pallas_call(
            functools.partial(penalty_kernel, scale, last_time),
            out_shape=field_shape,
            in_specs=[SMEM] + [VMEM] * 7,
            out_specs=VMEM,
            scratch_shapes=lag_scratch,
            compiler_params=SMALL,
        )(place, field, *fetched, lag_weights, local, other)
        second = with_pair(part, lambda i: n_series - 1 - i)
        total, low, *halos = pl.pallas_call(
            functools.partial(sum_kernel, ridge),
            out_shape=(field_shape, low_shape) + out_halos,
            in_specs=[SMEM] + [VMEM] * 3,
            out_specs=(VMEM,) * (2 + len(out_halos)),
            compiler_params=SMALL,
        )(place, part, second, field)
        return total, low, halos

    seen = observed == 1

    def fit(low):
        return jnp.where(seen, against(low, series_factors), 0.0)

    def back(rows_here):
        return jnp.dot(rows_here, series_factors, preferred_element_type=jnp.float32)

    low, *halos = pl.pallas_call(
        start_kernel,
        out_shape=(low_shape,) + halo_shapes,
        in_specs=[SMEM, VMEM],
        out_specs=(VMEM,) * 4,
        compiler_params=SMALL,
    )(place, time_factors)
    kept = jnp.where(seen, series_values, jnp.zeros((), jnp.bfloat16))
    local = back(kept) - back(fit(low).astype(jnp.bfloat16))
    power0, low, halos = finish(
        -penalty_weight, time_factors, halos, local, -ridge_weight, halo_shapes
    )

    def image(field, low, halos, out_halos):
        local = back(fit(low).astype(jnp.bfloat16))
        return finish(penalty_weight, field, halos, local, ridge_weight, out_halos)

    power1, low, halos = image(power0, low, halos, halo_shapes)
    power2, low, (many,) = image(power1, low, halos, last_shape)
    many = lax.ppermute(many, both, last_route)
    fitted = fit(low)
    squares = jnp.sum(fitted * fitted).reshape(1, 1)
    spread = pl.pallas_call(
        functools.partial(moments_kernel, 1.0 / n_series, last_time),
        out_shape=jax.ShapeDtypeStruct((everyone, 1, rank), jnp.float32),
        in_specs=[SMEM, SMEM] + [VMEM] * 5,
        out_specs=VMEM,
        scratch_shapes=lag_scratch,
        compiler_params=SMALL,
    )(place, squares, power0, power1, power2, many, lag_weights)
    gathered = lax.all_to_all(spread, both, split_axis=0, concat_axis=0, tiled=True)
    final, misfit = pl.pallas_call(
        update_kernel,
        out_shape=(field_shape, jax.ShapeDtypeStruct((n_tm, rows, rank), jnp.bfloat16)),
        in_specs=[VMEM] * 7,
        out_specs=(VMEM, VMEM),
        compiler_params=SMALL,
    )(gathered, time_factors, power0, power1, power2, series_values, series_factors)
    misfit = lax.all_to_all(misfit, "tm", split_axis=0, concat_axis=0, tiled=True)
    return final, misfit.reshape(n_tm * rows, rank)


def solution(mesh):
    placed = (P("tm", "series"), P("tm", "series"), P("series", None), P("tm", None), P())
    return jax.shard_map(
        on_device,
        mesh=mesh,
        in_specs=placed,
        out_specs=(P("tm", None), P(None, ("series", "tm"))),
        check_vma=False,
    )
```

```python
import functools

import jax
import jax.numpy as jnp
from jax import lax
from jax.experimental import pallas as pl
from jax.experimental.pallas import tpu as pltpu
from jax.sharding import PartitionSpec as P

SHORT = 24
SEASON = 168
LAGS = list(range(1, SHORT + 1)) + [SEASON]
MANY = 48
FEW = 24
FOLD = 16
EDGE = SEASON + 8
data_weight = 2.0
penalty_weight = 0.5
ridge_weight = 0.2

VMEM = pl.BlockSpec(memory_space=pltpu.VMEM)
SMEM = pl.BlockSpec(memory_space=pltpu.SMEM)
SMALL = pltpu.CompilerParams(vmem_limit_bytes=2 << 20)


def against(left_rows, factors):
    return lax.dot_general(
        left_rows, factors, (((1,), (1,)), ((), ())), preferred_element_type=jnp.float32
    )


def lag_product(place_ref, blocks, weights_ref, window, short, last_time):
    rank = weights_ref.shape[1]
    rows = window.shape[0] - 2 * EDGE
    first_time = place_ref[1]
    window[...] = jnp.zeros_like(window)
    for start, block in blocks:
        if not isinstance(start, int):
            start = pl.multiple_of(start, 8)
        window[pl.ds(start, block.shape[0]), :] = block

    def weight(number):
        return weights_ref[number : number + 1, :]

    def lagged(start, count):
        base = EDGE + start
        result = window[base : base + count, :]
        for number, lag in enumerate(LAGS):
            result = result - weight(number) * window[base - lag : base - lag + count, :]
        stamp = first_time + start + lax.broadcasted_iota(jnp.int32, (count, rank), 0)
        return jnp.where(stamp < last_time, result, 0.0)

    short[...] = lagged(0, rows + SHORT)
    result = short[0:rows, :] - weight(SHORT) * lagged(SEASON, rows)
    for number in range(SHORT):
        lag = LAGS[number]
        result = result - weight(number) * short[lag : lag + rows, :]
    return result


def penalty_kernel(
    scale, last_time, place_ref, field_ref, many_ref, few_ref, weights_ref, local_ref,
    part_ref, window, short,
):
    here = place_ref[0]
    many_at = jnp.where(
        here == 0, 0, jnp.where(here == 1, 368, jnp.where(here == 2, 48, 320))
    )
    blocks = [
        (EDGE, jnp.where(here == 0, field_ref[...], 0.0)),
        (many_at, many_ref[...]),
        (jnp.where(here == 3, 240, 152), few_ref[...]),
    ]
    product = lag_product(place_ref, blocks, weights_ref, window, short, last_time)
    part_ref[...] = data_weight * local_ref[...] + scale * product


def halo(here, field, many_ref, few_ref):
    rows = field.shape[0]
    late = jnp.logical_or(here == 0, here == 3)
    many_ref[...] = jnp.where(late, field[rows - MANY :], field[:MANY])
    few_ref[...] = jnp.where(here == 2, field[rows - FEW :], field[:FEW])


def start_kernel(place_ref, field_ref, low_ref, many_ref, few_ref):
    field = field_ref[...]
    low_ref[...] = field.astype(jnp.bfloat16)
    halo(place_ref[0], field, many_ref, few_ref)


def sum_kernel(
    scale, place_ref, own_ref, first_ref, second_ref, third_ref, field_ref,
    total_ref, low_ref, many_ref, few_ref,
):
    here = place_ref[0]
    total = (own_ref[...] + second_ref[...]) + (first_ref[...] + third_ref[...])
    total = total + scale * field_ref[...]
    total_ref[...] = total
    low_ref[...] = total.astype(jnp.bfloat16)
    halo(here, total, many_ref, few_ref)


def moments_kernel(
    share, last_time, place_ref, squares_ref, zero_ref, one_ref, two_ref, many_ref,
    weights_ref, spread_ref, window, short,
):
    zero, one, two = zero_ref[...], one_ref[...], two_ref[...]
    here = place_ref[0]
    many_at = jnp.where(here == 0, 0, jnp.where(here == 2, 48, 128))
    blocks = [
        (EDGE, jnp.where(here == 1, two, 0.0)),
        (many_at, jnp.where(here == 1, 0.0, 2.0 * many_ref[...])),
    ]
    product = lag_product(place_ref, blocks, weights_ref, window, short, last_time)

    def inner(left, right):
        return jnp.sum(left * right, axis=0, keepdims=True)

    tile = jnp.concatenate(
        [
            share * inner(zero, zero),
            share * inner(zero, one),
            share * inner(zero, two),
            share * inner(one, one),
            share * inner(one, two),
            share * inner(two, two),
            penalty_weight * inner(two, product),
            jnp.zeros_like(zero[:1]),
        ],
        axis=0,
    )
    for shift in (64, 32, 16):
        tile = tile + pltpu.roll(tile, shift, 1)
    group = lax.broadcasted_iota(jnp.int32, tile.shape, 1) // FOLD
    number = lax.broadcasted_iota(jnp.int32, tile.shape, 0)
    packed = jnp.sum(jnp.where(group == number, tile, 0.0), axis=0, keepdims=True)
    lane = lax.broadcasted_iota(jnp.int32, packed.shape, 1)
    packed = packed + jnp.where(lane == 6 * FOLD, data_weight * squares_ref[0, 0], 0.0)
    spread_ref[...] = jnp.broadcast_to(packed[None], spread_ref.shape)


def update_kernel(
    gathered_ref, start_ref, zero_ref, one_ref, two_ref, values_ref, factors_ref,
    final_ref, misfit_ref,
):
    total = jnp.sum(gathered_ref[...], axis=0)
    lane = lax.broadcasted_iota(jnp.int32, total.shape, 1)

    def pick(number):
        return jnp.sum(jnp.where(lane // FOLD == number, total, 0.0), axis=1, keepdims=True)

    m00, m01, m02, m11, m12, m22, m23 = [pick(number) for number in range(7)]
    m23 = m23 + ridge_weight * m22
    alpha0 = m00 / m01
    norm1 = m00 - 2.0 * alpha0 * m01 + alpha0 * alpha0 * m11
    g0 = 1.0 + norm1 / m00
    curvature1 = g0 * g0 * m01 - g0 * alpha0 * (m02 + m11) + alpha0 * alpha0 * m12
    alpha1 = norm1 / curvature1
    a = -(alpha0 + alpha1 * g0)
    b = alpha0 * alpha1
    norm2 = m00 + a * a * m11 + b * b * m22 + 2.0 * (a * m01 + b * m02 + a * b * m12)
    beta1 = norm2 / norm1
    c = 1.0 + beta1 * g0
    d = a - beta1 * alpha0
    curvature2 = (
        c * c * m01
        + c * d * (m02 + m11)
        + 2.0 * c * b * m12
        + d * d * m12
        + 2.0 * d * b * m22
        + b * b * m23
    )
    alpha2 = norm2 / curvature2
    k0 = alpha0 + alpha1 * g0 + alpha2 * c
    k1 = alpha2 * d - alpha1 * alpha0
    k2 = alpha2 * b
    final = start_ref[...] + (k0 * zero_ref[...] + k1 * one_ref[...] + k2 * two_ref[...])
    final_ref[...] = final
    low = final.astype(jnp.bfloat16)
    lanes = misfit_ref.shape[2]
    for first in range(0, values_ref.shape[1], 2 * lanes):
        columns = slice(first, first + 2 * lanes)
        fitted = against(low, factors_ref[columns, :])
        block = (values_ref[:, columns].astype(jnp.float32) - fitted).astype(jnp.bfloat16)
        misfit_ref[first // lanes] = block[:, :lanes]
        misfit_ref[first // lanes + 1] = block[:, lanes:]


def on_device(series_values, observed, series_factors, time_factors, lag_weights):
    rows, rank = time_factors.shape
    n_tm = lax.axis_size("tm")
    n_series = lax.axis_size("series")
    everyone = n_tm * n_series
    last_time = n_tm * rows
    here = lax.axis_index("series")
    place = jnp.stack([here, lax.axis_index("tm") * rows]).astype(jnp.int32)
    field_shape = jax.ShapeDtypeStruct((rows, rank), jnp.float32)
    many_shape = jax.ShapeDtypeStruct((MANY, rank), jnp.float32)
    few_shape = jax.ShapeDtypeStruct((FEW, rank), jnp.float32)
    low_shape = jax.ShapeDtypeStruct((rows, rank), jnp.bfloat16)
    lag_scratch = [
        pltpu.VMEM((2 * EDGE + rows, rank), jnp.float32),
        pltpu.VMEM((rows + SHORT, rank), jnp.float32),
    ]

    def route(steps):
        pairs = []
        for column, step in enumerate(steps):
            if step is None:
                continue
            for source in range(n_tm):
                target = source + step
                if 0 <= target < n_tm:
                    pairs.append((source * n_series + column, target * n_series + column))
        return pairs

    many_route = route([3, -3, 2, -2])
    few_route = route([None, None, 1, -1])
    last_route = route([3, None, 2, 1])
    both = ("tm", "series")

    def fetch(many, few, local):
        few, local = lax.optimization_barrier((few, local))
        few = lax.ppermute(few, both, few_route)
        return lax.ppermute(many, both, many_route), few, local

    def penalty(scale, field, many, few, local):
        return pl.pallas_call(
            functools.partial(penalty_kernel, scale, last_time),
            out_shape=field_shape,
            in_specs=[SMEM] + [VMEM] * 5,
            out_specs=VMEM,
            scratch_shapes=lag_scratch,
            compiler_params=SMALL,
        )(place, field, many, few, lag_weights, local)

    def series_sum(scale, part, field):
        def moved(distance):
            pairs = [(i, (i + distance) % n_series) for i in range(n_series)]
            return lax.ppermute(part, "series", pairs)

        first, third = moved(1), moved(3)
        second = moved(2)
        return pl.pallas_call(
            functools.partial(sum_kernel, scale),
            out_shape=(
                field_shape,
                low_shape,
                many_shape,
                few_shape,
            ),
            in_specs=[SMEM] + [VMEM] * 5,
            out_specs=(VMEM,) * 4,
            compiler_params=SMALL,
        )(place, part, first, second, third, field)

    seen = observed == 1

    def fit(low):
        return jnp.where(seen, against(low, series_factors), 0.0)

    def back(rows_here):
        return jnp.dot(rows_here, series_factors, preferred_element_type=jnp.float32)

    low, many, few = pl.pallas_call(
        start_kernel,
        out_shape=(low_shape, many_shape, few_shape),
        in_specs=[SMEM, VMEM],
        out_specs=(VMEM,) * 3,
        compiler_params=SMALL,
    )(place, time_factors)
    kept = jnp.where(seen, series_values, jnp.zeros((), jnp.bfloat16))
    local = back(kept) - back(fit(low).astype(jnp.bfloat16))
    many, few, local = fetch(many, few, local)
    part = penalty(-penalty_weight, time_factors, many, few, local)
    power0, low, many, few = series_sum(-ridge_weight, part, time_factors)

    def image(field, low, many, few):
        local = back(fit(low).astype(jnp.bfloat16))
        many, few, local = fetch(many, few, local)
        part = penalty(penalty_weight, field, many, few, local)
        return series_sum(ridge_weight, part, field)

    power1, low, many, few = image(power0, low, many, few)
    power2, low, many, few = image(power1, low, many, few)
    many = lax.ppermute(many, both, last_route)
    fitted = fit(low)
    squares = jnp.sum(fitted * fitted).reshape(1, 1)
    spread = pl.pallas_call(
        functools.partial(moments_kernel, 1.0 / n_series, last_time),
        out_shape=jax.ShapeDtypeStruct((everyone, 1, rank), jnp.float32),
        in_specs=[SMEM, SMEM] + [VMEM] * 5,
        out_specs=VMEM,
        scratch_shapes=lag_scratch,
        compiler_params=SMALL,
    )(place, squares, power0, power1, power2, many, lag_weights)
    gathered = lax.all_to_all(spread, both, split_axis=0, concat_axis=0, tiled=True)
    final, misfit = pl.pallas_call(
        update_kernel,
        out_shape=(field_shape, jax.ShapeDtypeStruct((n_tm, rows, rank), jnp.bfloat16)),
        in_specs=[VMEM] * 7,
        out_specs=(VMEM, VMEM),
        compiler_params=SMALL,
    )(gathered, time_factors, power0, power1, power2, series_values, series_factors)
    misfit = lax.all_to_all(misfit, "tm", split_axis=0, concat_axis=0, tiled=True)
    return final, misfit.reshape(n_tm * rows, rank)


def solution(mesh):
    placed = (P("tm", "series"), P("tm", "series"), P("series", None), P("tm", None), P())
    return jax.shard_map(
        on_device,
        mesh=mesh,
        in_specs=placed,
        out_specs=(P("tm", None), P(None, ("series", "tm"))),
        check_vma=False,
    )
```

```python
import functools

import jax
import jax.numpy as jnp
from jax import lax
from jax.experimental import pallas as pl
from jax.experimental.pallas import tpu as pltpu
from jax.sharding import PartitionSpec as P

SHORT = 24
SEASON = 168
LAGS = list(range(1, SHORT + 1)) + [SEASON]
MANY = 48
FEW = 24
EDGE = SEASON + 8
data_weight = 2.0
penalty_weight = 0.5
ridge_weight = 0.2

VMEM = pl.BlockSpec(memory_space=pltpu.VMEM)
SMEM = pl.BlockSpec(memory_space=pltpu.SMEM)
SMALL = pltpu.CompilerParams(vmem_limit_bytes=2 << 20)


def against(left_rows, factors):
    return lax.dot_general(
        left_rows, factors, (((1,), (1,)), ((), ())), preferred_element_type=jnp.float32
    )


def lag_product(place_ref, blocks, weights_ref, window, short, last_time):
    rank = weights_ref.shape[1]
    rows = window.shape[0] - 2 * EDGE
    first_time = place_ref[1]
    window[...] = jnp.zeros_like(window)
    for start, block in blocks:
        if not isinstance(start, int):
            start = pl.multiple_of(start, 8)
        window[pl.ds(start, block.shape[0]), :] = block

    def weight(number):
        return weights_ref[number : number + 1, :]

    def lagged(start, count):
        base = EDGE + start
        result = window[base : base + count, :]
        for number, lag in enumerate(LAGS):
            result = result - weight(number) * window[base - lag : base - lag + count, :]
        stamp = first_time + start + lax.broadcasted_iota(jnp.int32, (count, rank), 0)
        return jnp.where(stamp < last_time, result, 0.0)

    short[...] = lagged(0, rows + SHORT)
    result = short[0:rows, :] - weight(SHORT) * lagged(SEASON, rows)
    for number in range(SHORT):
        lag = LAGS[number]
        result = result - weight(number) * short[lag : lag + rows, :]
    return result


def penalty_kernel(
    scale, last_time, place_ref, field_ref, many_ref, few_ref, weights_ref, local_ref,
    part_ref, window, short,
):
    here = place_ref[0]
    many_at = jnp.where(
        here == 0, 0, jnp.where(here == 1, 368, jnp.where(here == 2, 48, 320))
    )
    blocks = [
        (EDGE, jnp.where(here == 0, field_ref[...], 0.0)),
        (many_at, many_ref[...].astype(jnp.float32)),
        (jnp.where(here == 3, 240, 152), few_ref[...].astype(jnp.float32)),
    ]
    product = lag_product(place_ref, blocks, weights_ref, window, short, last_time)
    part_ref[...] = data_weight * local_ref[...] + scale * product


def halo(here, field, many_ref, few_ref=None):
    rows = field.shape[0]
    late = jnp.logical_or(here == 0, here == 3)
    many = jnp.where(late, field[rows - MANY :], field[:MANY])
    many_ref[...] = many.astype(many_ref.dtype)
    if few_ref is not None:
        few = jnp.where(here == 2, field[rows - FEW :], field[:FEW])
        few_ref[...] = few.astype(few_ref.dtype)


def start_kernel(place_ref, field_ref, low_ref, many_ref, few_ref):
    field = field_ref[...]
    low_ref[...] = field.astype(jnp.bfloat16)
    halo(place_ref[0], field, many_ref, few_ref)


def sum_kernel(
    scale, place_ref, own_ref, first_ref, second_ref, third_ref, field_ref,
    total_ref, low_ref, *halo_refs,
):
    here = place_ref[0]
    total = (own_ref[...] + second_ref[...]) + (first_ref[...] + third_ref[...])
    total = total + scale * field_ref[...]
    total_ref[...] = total
    low_ref[...] = total.astype(jnp.bfloat16)
    halo(here, total, *halo_refs)


def place_sums(sums, first, rank):
    lane = lax.broadcasted_iota(jnp.int32, (1, rank), 1)
    packed = jnp.zeros((1, rank), jnp.float32)
    for number, value in enumerate(sums):
        packed = jnp.where(lane == first + number, value, packed)
    return packed


def inner(left, right):
    return jnp.sum(jnp.sum(left * right, axis=0, keepdims=True), axis=1, keepdims=True)


def products_kernel(share, zero_ref, one_ref, two_ref, packed_ref):
    zero, one, two = zero_ref[...], one_ref[...], two_ref[...]
    sums = [
        inner(zero, zero),
        inner(zero, one),
        inner(zero, two),
        inner(one, one),
        inner(one, two),
        inner(two, two),
    ]
    packed = share * place_sums(sums, 0, zero.shape[1])
    packed_ref[...] = jnp.broadcast_to(packed, packed_ref.shape)


def moments_kernel(
    last_time, place_ref, squares_ref, packed_ref, two_ref, many_ref,
    weights_ref, spread_ref, window, short,
):
    two = two_ref[...]
    here = place_ref[0]
    many_at = jnp.where(here == 0, 0, jnp.where(here == 2, 48, 128))
    blocks = [
        (EDGE, jnp.where(here == 1, two, 0.0)),
        (many_at, jnp.where(here == 1, 0.0, 2.0 * many_ref[...].astype(jnp.float32))),
    ]
    product = lag_product(place_ref, blocks, weights_ref, window, short, last_time)
    quadratic = data_weight * squares_ref[0, 0] + penalty_weight * inner(two, product)
    packed = packed_ref[0:1, :] + place_sums([quadratic], 6, two.shape[1])
    spread_ref[...] = jnp.broadcast_to(packed[None], spread_ref.shape)


def update_kernel(
    gathered_ref, start_ref, zero_ref, one_ref, two_ref, values_ref, factors_ref,
    final_ref, misfit_ref,
):
    total = jnp.sum(gathered_ref[...], axis=0)
    lane = lax.broadcasted_iota(jnp.int32, total.shape, 1)

    def pick(number):
        return jnp.sum(jnp.where(lane == number, total, 0.0), axis=1, keepdims=True)

    m00, m01, m02, m11, m12, m22, m23 = [pick(number) for number in range(7)]
    m23 = m23 + ridge_weight * m22
    alpha0 = m00 / m01
    norm1 = m00 - 2.0 * alpha0 * m01 + alpha0 * alpha0 * m11
    g0 = 1.0 + norm1 / m00
    curvature1 = g0 * g0 * m01 - g0 * alpha0 * (m02 + m11) + alpha0 * alpha0 * m12
    alpha1 = norm1 / curvature1
    a = -(alpha0 + alpha1 * g0)
    b = alpha0 * alpha1
    norm2 = m00 + a * a * m11 + b * b * m22 + 2.0 * (a * m01 + b * m02 + a * b * m12)
    beta1 = norm2 / norm1
    c = 1.0 + beta1 * g0
    d = a - beta1 * alpha0
    curvature2 = (
        c * c * m01
        + c * d * (m02 + m11)
        + 2.0 * c * b * m12
        + d * d * m12
        + 2.0 * d * b * m22
        + b * b * m23
    )
    alpha2 = norm2 / curvature2
    k0 = alpha0 + alpha1 * g0 + alpha2 * c
    k1 = alpha2 * d - alpha1 * alpha0
    k2 = alpha2 * b
    final = start_ref[...] + (k0 * zero_ref[...] + k1 * one_ref[...] + k2 * two_ref[...])
    final_ref[...] = final
    low = final.astype(jnp.bfloat16)
    lanes = misfit_ref.shape[2]
    for first in range(0, values_ref.shape[1], 2 * lanes):
        columns = slice(first, first + 2 * lanes)
        fitted = against(low, factors_ref[columns, :])
        block = (values_ref[:, columns].astype(jnp.float32) - fitted).astype(jnp.bfloat16)
        misfit_ref[first // lanes] = block[:, :lanes]
        misfit_ref[first // lanes + 1] = block[:, lanes:]


def on_device(series_values, observed, series_factors, time_factors, lag_weights):
    rows, rank = time_factors.shape
    n_tm = lax.axis_size("tm")
    n_series = lax.axis_size("series")
    everyone = n_tm * n_series
    last_time = n_tm * rows
    here = lax.axis_index("series")
    place = jnp.stack([here, lax.axis_index("tm") * rows]).astype(jnp.int32)
    field_shape = jax.ShapeDtypeStruct((rows, rank), jnp.float32)
    many_shape = jax.ShapeDtypeStruct((MANY, rank), jnp.bfloat16)
    few_shape = jax.ShapeDtypeStruct((FEW, rank), jnp.bfloat16)
    halo_shapes = (many_shape, few_shape)
    low_shape = jax.ShapeDtypeStruct((rows, rank), jnp.bfloat16)
    lag_scratch = [
        pltpu.VMEM((2 * EDGE + rows, rank), jnp.float32),
        pltpu.VMEM((rows + SHORT, rank), jnp.float32),
    ]

    def route(steps):
        pairs = []
        for column, step in enumerate(steps):
            if step is None:
                continue
            for source in range(n_tm):
                target = source + step
                if 0 <= target < n_tm:
                    pairs.append((source * n_series + column, target * n_series + column))
        return pairs

    many_route = route([3, -3, 2, -2])
    few_route = route([None, None, 1, -1])
    last_route = route([3, None, 2, 1])
    both = ("tm", "series")

    def fetch(many, few):
        few = lax.ppermute(few, both, few_route)
        return lax.ppermute(many, both, many_route), few

    def penalty(scale, field, many, few, local):
        return pl.pallas_call(
            functools.partial(penalty_kernel, scale, last_time),
            out_shape=field_shape,
            in_specs=[SMEM] + [VMEM] * 5,
            out_specs=VMEM,
            scratch_shapes=lag_scratch,
            compiler_params=SMALL,
        )(place, field, many, few, lag_weights, local)

    def series_sum(scale, part, field, out_halos):
        def moved(distance):
            pairs = [(i, (i + distance) % n_series) for i in range(n_series)]
            return lax.ppermute(part, "series", pairs)

        first, third = moved(1), moved(3)
        second = moved(2)
        return pl.pallas_call(
            functools.partial(sum_kernel, scale),
            out_shape=(field_shape, low_shape) + out_halos,
            in_specs=[SMEM] + [VMEM] * 5,
            out_specs=(VMEM,) * (2 + len(out_halos)),
            compiler_params=SMALL,
        )(place, part, first, second, third, field)

    seen = observed == 1

    def fit(low):
        return jnp.where(seen, against(low, series_factors), 0.0)

    def back(rows_here):
        return jnp.dot(rows_here, series_factors, preferred_element_type=jnp.float32)

    low, many, few = pl.pallas_call(
        start_kernel,
        out_shape=(low_shape, many_shape, few_shape),
        in_specs=[SMEM, VMEM],
        out_specs=(VMEM,) * 3,
        compiler_params=SMALL,
    )(place, time_factors)
    many, few = fetch(many, few)
    kept = jnp.where(seen, series_values, jnp.zeros((), jnp.bfloat16))
    local = back(kept) - back(fit(low).astype(jnp.bfloat16))
    part = penalty(-penalty_weight, time_factors, many, few, local)
    power0, low, many, few = series_sum(-ridge_weight, part, time_factors, halo_shapes)

    def image(field, low, many, few, out_halos):
        many, few = fetch(many, few)
        local = back(fit(low).astype(jnp.bfloat16))
        part = penalty(penalty_weight, field, many, few, local)
        return series_sum(ridge_weight, part, field, out_halos)

    power1, low, many, few = image(power0, low, many, few, halo_shapes)
    power2, low, many = image(power1, low, many, few, (many_shape,))
    many = lax.ppermute(many, both, last_route)
    fitted = fit(low)
    squares = jnp.sum(fitted * fitted).reshape(1, 1)
    packed = pl.pallas_call(
        functools.partial(products_kernel, 1.0 / n_series),
        out_shape=jax.ShapeDtypeStruct((8, rank), jnp.float32),
        in_specs=[VMEM] * 3,
        out_specs=VMEM,
        compiler_params=SMALL,
    )(power0, power1, power2)
    spread = pl.pallas_call(
        functools.partial(moments_kernel, last_time),
        out_shape=jax.ShapeDtypeStruct((everyone, 1, rank), jnp.float32),
        in_specs=[SMEM, SMEM] + [VMEM] * 4,
        out_specs=VMEM,
        scratch_shapes=lag_scratch,
        compiler_params=SMALL,
    )(place, squares, packed, power2, many, lag_weights)
    gathered = lax.all_to_all(spread, both, split_axis=0, concat_axis=0, tiled=True)
    final, misfit = pl.pallas_call(
        update_kernel,
        out_shape=(field_shape, jax.ShapeDtypeStruct((n_tm, rows, rank), jnp.bfloat16)),
        in_specs=[VMEM] * 7,
        out_specs=(VMEM, VMEM),
        compiler_params=SMALL,
    )(gathered, time_factors, power0, power1, power2, series_values, series_factors)
    misfit = lax.all_to_all(misfit, "tm", split_axis=0, concat_axis=0, tiled=True)
    return final, misfit.reshape(n_tm * rows, rank)


def solution(mesh):
    placed = (P("tm", "series"), P("tm", "series"), P("series", None), P("tm", None), P())
    return jax.shard_map(
        on_device,
        mesh=mesh,
        in_specs=placed,
        out_specs=(P("tm", None), P(None, ("series", "tm"))),
        check_vma=False,
    )
```

```python
import functools

import jax
import jax.numpy as jnp
from jax import lax
from jax.experimental import pallas as pl
from jax.experimental.pallas import tpu as pltpu
from jax.sharding import PartitionSpec as P

SHORT = 24
SEASON = 168
LAGS = list(range(1, SHORT + 1)) + [SEASON]
MANY = 48
FEW = 24
EDGE = SEASON + 8
data_weight = 2.0
penalty_weight = 0.5
ridge_weight = 0.2

VMEM = pl.BlockSpec(memory_space=pltpu.VMEM)
SMALL = pltpu.CompilerParams(vmem_limit_bytes=2 << 20)


def against(left_rows, factors):
    return lax.dot_general(
        left_rows, factors, (((1,), (1,)), ((), ())), preferred_element_type=jnp.float32
    )


def lag_product(blocks, weights_ref, window, short, last_time):
    rank = weights_ref.shape[1]
    rows = window.shape[0] - 2 * EDGE
    first_time = lax.axis_index("tm") * rows
    window[...] = jnp.zeros_like(window)
    for start, block in blocks:
        if not isinstance(start, int):
            start = pl.multiple_of(start, 8)
        window[pl.ds(start, block.shape[0]), :] = block

    def weight(number):
        return weights_ref[number : number + 1, :]

    def lagged(start, count):
        base = EDGE + start
        result = window[base : base + count, :]
        for number, lag in enumerate(LAGS):
            result = result - weight(number) * window[base - lag : base - lag + count, :]
        stamp = first_time + start + lax.broadcasted_iota(jnp.int32, (count, rank), 0)
        return jnp.where(stamp < last_time, result, 0.0)

    short[...] = lagged(0, rows + SHORT)
    result = short[0:rows, :] - weight(SHORT) * lagged(SEASON, rows)
    for number in range(SHORT):
        lag = LAGS[number]
        result = result - weight(number) * short[lag : lag + rows, :]
    return result


def penalty_kernel(
    scale, last_time, field_ref, many_ref, few_ref, weights_ref, local_ref,
    part_ref, window, short,
):
    here = lax.axis_index("series")
    many_at = jnp.where(
        here == 0, 0, jnp.where(here == 1, 368, jnp.where(here == 2, 48, 320))
    )
    blocks = [
        (EDGE, jnp.where(here == 0, field_ref[...], 0.0)),
        (many_at, many_ref[...].astype(jnp.float32)),
        (jnp.where(here == 3, 240, 152), few_ref[...].astype(jnp.float32)),
    ]
    product = lag_product(blocks, weights_ref, window, short, last_time)
    part_ref[...] = data_weight * local_ref[...] + scale * product


def halo(here, field, many_ref, few_ref=None):
    rows = field.shape[0]
    late = jnp.logical_or(here == 0, here == 3)
    many = jnp.where(late, field[rows - MANY :], field[:MANY])
    many_ref[...] = many.astype(many_ref.dtype)
    if few_ref is not None:
        few = jnp.where(here == 2, field[rows - FEW :], field[:FEW])
        few_ref[...] = few.astype(few_ref.dtype)


def start_kernel(field_ref, low_ref, many_ref, few_ref):
    field = field_ref[...]
    low_ref[...] = field.astype(jnp.bfloat16)
    halo(lax.axis_index("series"), field, many_ref, few_ref)


def sum_kernel(
    scale, own_ref, first_ref, second_ref, third_ref, field_ref,
    total_ref, low_ref, *halo_refs,
):
    here = lax.axis_index("series")
    total = (own_ref[...] + second_ref[...]) + (first_ref[...] + third_ref[...])
    total = total + scale * field_ref[...]
    total_ref[...] = total
    low_ref[...] = total.astype(jnp.bfloat16)
    halo(here, total, *halo_refs)


def place_sums(sums, first, rank):
    lane = lax.broadcasted_iota(jnp.int32, (1, rank), 1)
    packed = jnp.zeros((1, rank), jnp.float32)
    for number, value in enumerate(sums):
        packed = jnp.where(lane == first + number, value, packed)
    return packed


def inner(left, right):
    return jnp.sum(jnp.sum(left * right, axis=0, keepdims=True), axis=1, keepdims=True)


def products_kernel(share, squares_ref, zero_ref, one_ref, two_ref, packed_ref):
    zero, one, two = zero_ref[...], one_ref[...], two_ref[...]
    sums = [
        inner(zero, zero),
        inner(zero, one),
        inner(zero, two),
        inner(one, one),
        inner(one, two),
        inner(two, two),
    ]
    squares = jnp.sum(squares_ref[...], axis=1, keepdims=True)
    packed = share * place_sums(sums, 0, zero.shape[1])
    packed = packed + place_sums([data_weight * squares], len(sums), zero.shape[1])
    packed_ref[...] = jnp.broadcast_to(packed, packed_ref.shape)


def moments_kernel(
    last_time, packed_ref, two_ref, many_ref,
    weights_ref, spread_ref, window, short,
):
    two = two_ref[...]
    here = lax.axis_index("series")
    many_at = jnp.where(here == 0, 0, jnp.where(here == 2, 48, 128))
    blocks = [
        (EDGE, jnp.where(here == 1, two, 0.0)),
        (many_at, jnp.where(here == 1, 0.0, 2.0 * many_ref[...].astype(jnp.float32))),
    ]
    product = lag_product(blocks, weights_ref, window, short, last_time)
    quadratic = penalty_weight * inner(two, product)
    packed = packed_ref[0:1, :] + place_sums([quadratic], 6, two.shape[1])
    spread_ref[...] = jnp.broadcast_to(packed[None], spread_ref.shape)


def update_kernel(
    gathered_ref, start_ref, zero_ref, one_ref, two_ref, values_ref, factors_ref,
    final_ref, misfit_ref,
):
    total = jnp.sum(gathered_ref[...], axis=0)
    lane = lax.broadcasted_iota(jnp.int32, total.shape, 1)

    def pick(number):
        return jnp.sum(jnp.where(lane == number, total, 0.0), axis=1, keepdims=True)

    m00, m01, m02, m11, m12, m22, m23 = [pick(number) for number in range(7)]
    m23 = m23 + ridge_weight * m22
    alpha0 = m00 / m01
    norm1 = m00 - 2.0 * alpha0 * m01 + alpha0 * alpha0 * m11
    g0 = 1.0 + norm1 / m00
    curvature1 = g0 * g0 * m01 - g0 * alpha0 * (m02 + m11) + alpha0 * alpha0 * m12
    alpha1 = norm1 / curvature1
    a = -(alpha0 + alpha1 * g0)
    b = alpha0 * alpha1
    norm2 = m00 + a * a * m11 + b * b * m22 + 2.0 * (a * m01 + b * m02 + a * b * m12)
    beta1 = norm2 / norm1
    c = 1.0 + beta1 * g0
    d = a - beta1 * alpha0
    curvature2 = (
        c * c * m01
        + c * d * (m02 + m11)
        + 2.0 * c * b * m12
        + d * d * m12
        + 2.0 * d * b * m22
        + b * b * m23
    )
    alpha2 = norm2 / curvature2
    k0 = alpha0 + alpha1 * g0 + alpha2 * c
    k1 = alpha2 * d - alpha1 * alpha0
    k2 = alpha2 * b
    final = start_ref[...] + (k0 * zero_ref[...] + k1 * one_ref[...] + k2 * two_ref[...])
    final_ref[...] = final
    low = final.astype(jnp.bfloat16)
    lanes = misfit_ref.shape[2]
    for first in range(0, values_ref.shape[1], 2 * lanes):
        columns = slice(first, first + 2 * lanes)
        fitted = against(low, factors_ref[columns, :])
        block = (values_ref[:, columns].astype(jnp.float32) - fitted).astype(jnp.bfloat16)
        misfit_ref[first // lanes] = block[:, :lanes]
        misfit_ref[first // lanes + 1] = block[:, lanes:]


def on_device(series_values, observed, series_factors, time_factors, lag_weights):
    rows, rank = time_factors.shape
    n_tm = lax.axis_size("tm")
    n_series = lax.axis_size("series")
    everyone = n_tm * n_series
    last_time = n_tm * rows
    field_shape = jax.ShapeDtypeStruct((rows, rank), jnp.float32)
    many_shape = jax.ShapeDtypeStruct((MANY, rank), jnp.bfloat16)
    few_shape = jax.ShapeDtypeStruct((FEW, rank), jnp.bfloat16)
    halo_shapes = (many_shape, few_shape)
    low_shape = jax.ShapeDtypeStruct((rows, rank), jnp.bfloat16)
    lag_scratch = [
        pltpu.VMEM((2 * EDGE + rows, rank), jnp.float32),
        pltpu.VMEM((rows + SHORT, rank), jnp.float32),
    ]

    def route(steps):
        pairs = []
        for column, step in enumerate(steps):
            if step is None:
                continue
            for source in range(n_tm):
                target = source + step
                if 0 <= target < n_tm:
                    pairs.append((source * n_series + column, target * n_series + column))
        return pairs

    many_route = route([3, -3, 2, -2])
    few_route = route([None, None, 1, -1])
    last_route = route([3, None, 2, 1])
    both = ("tm", "series")

    def fetch(many, few):
        few = lax.ppermute(few, both, few_route)
        return lax.ppermute(many, both, many_route), few

    def penalty(scale, field, many, few, local):
        return pl.pallas_call(
            functools.partial(penalty_kernel, scale, last_time),
            out_shape=field_shape,
            in_specs=[VMEM] * 5,
            out_specs=VMEM,
            scratch_shapes=lag_scratch,
            compiler_params=SMALL,
        )(field, many, few, lag_weights, local)

    def series_sum(scale, part, field, out_halos):
        def moved(distance):
            pairs = [(i, (i + distance) % n_series) for i in range(n_series)]
            return lax.ppermute(part, "series", pairs)

        first, third = moved(1), moved(3)
        second = moved(2)
        return pl.pallas_call(
            functools.partial(sum_kernel, scale),
            out_shape=(field_shape, low_shape) + out_halos,
            in_specs=[VMEM] * 5,
            out_specs=(VMEM,) * (2 + len(out_halos)),
            compiler_params=SMALL,
        )(part, first, second, third, field)

    seen = observed == 1

    def fit(low):
        return jnp.where(seen, against(low, series_factors), 0.0)

    def back(rows_here):
        return jnp.dot(rows_here, series_factors, preferred_element_type=jnp.float32)

    low, many, few = pl.pallas_call(
        start_kernel,
        out_shape=(low_shape, many_shape, few_shape),
        in_specs=[VMEM],
        out_specs=(VMEM,) * 3,
        compiler_params=SMALL,
    )(time_factors)
    many, few = fetch(many, few)
    kept = jnp.where(seen, series_values, jnp.zeros((), jnp.bfloat16))
    local = back(kept) - back(fit(low).astype(jnp.bfloat16))
    part = penalty(-penalty_weight, time_factors, many, few, local)
    power0, low, many, few = series_sum(-ridge_weight, part, time_factors, halo_shapes)

    def image(field, low, many, few, out_halos):
        many, few = fetch(many, few)
        local = back(fit(low).astype(jnp.bfloat16))
        part = penalty(penalty_weight, field, many, few, local)
        return series_sum(ridge_weight, part, field, out_halos)

    power1, low, many, few = image(power0, low, many, few, halo_shapes)
    power2, low, many = image(power1, low, many, few, (many_shape,))
    many = lax.ppermute(many, both, last_route)
    fitted = fit(low)
    squares = jnp.sum(fitted * fitted, axis=0, keepdims=True)
    packed = pl.pallas_call(
        functools.partial(products_kernel, 1.0 / n_series),
        out_shape=jax.ShapeDtypeStruct((8, rank), jnp.float32),
        in_specs=[VMEM] * 4,
        out_specs=VMEM,
        compiler_params=SMALL,
    )(squares, power0, power1, power2)
    spread = pl.pallas_call(
        functools.partial(moments_kernel, last_time),
        out_shape=jax.ShapeDtypeStruct((everyone, 1, rank), jnp.float32),
        in_specs=[VMEM] * 4,
        out_specs=VMEM,
        scratch_shapes=lag_scratch,
        compiler_params=SMALL,
    )(packed, power2, many, lag_weights)
    gathered = lax.all_to_all(spread, both, split_axis=0, concat_axis=0, tiled=True)
    final, misfit = pl.pallas_call(
        update_kernel,
        out_shape=(field_shape, jax.ShapeDtypeStruct((n_tm, rows, rank), jnp.bfloat16)),
        in_specs=[VMEM] * 7,
        out_specs=(VMEM, VMEM),
        compiler_params=SMALL,
    )(gathered, time_factors, power0, power1, power2, series_values, series_factors)
    misfit = lax.all_to_all(misfit, "tm", split_axis=0, concat_axis=0, tiled=True)
    return final, misfit.reshape(n_tm * rows, rank)


def solution(mesh):
    placed = (P("tm", "series"), P("tm", "series"), P("series", None), P("tm", None), P())
    return jax.shard_map(
        on_device,
        mesh=mesh,
        in_specs=placed,
        out_specs=(P("tm", None), P(None, ("series", "tm"))),
        check_vma=False,
    )
```

```python
import functools

import jax
import jax.numpy as jnp
from jax import lax
from jax.experimental import pallas as pl
from jax.experimental.pallas import tpu as pltpu
from jax.sharding import PartitionSpec as P

SHORT = 24
SEASON = 168
LAGS = list(range(1, SHORT + 1)) + [SEASON]
MANY = 48
FEW = 48
EDGE = SEASON + 8
data_weight = 2.0
penalty_weight = 0.5
ridge_weight = 0.2

VMEM = pl.BlockSpec(memory_space=pltpu.VMEM)
SMALL = pltpu.CompilerParams(vmem_limit_bytes=2 << 20)


def against(left_rows, factors):
    return lax.dot_general(
        left_rows, factors, (((1,), (1,)), ((), ())), preferred_element_type=jnp.float32
    )


def lag_product(blocks, weights_ref, window, short, last_time):
    rank = weights_ref.shape[1]
    rows = window.shape[0] - 2 * EDGE
    first_time = lax.axis_index("tm") * rows
    window[...] = jnp.zeros_like(window)
    for start, block in blocks:
        if not isinstance(start, int):
            start = pl.multiple_of(start, 8)
        window[pl.ds(start, block.shape[0]), :] = block

    def weight(number):
        return weights_ref[number : number + 1, :]

    def lagged(start, count):
        base = EDGE + start
        result = window[base : base + count, :]
        for number, lag in enumerate(LAGS):
            result = result - weight(number) * window[base - lag : base - lag + count, :]
        stamp = first_time + start + lax.broadcasted_iota(jnp.int32, (count, rank), 0)
        return jnp.where(stamp < last_time, result, 0.0)

    short[...] = lagged(0, rows + SHORT)
    result = short[0:rows, :] - weight(SHORT) * lagged(SEASON, rows)
    for number in range(SHORT):
        lag = LAGS[number]
        result = result - weight(number) * short[lag : lag + rows, :]
    return result


def penalty_kernel(
    scale, last_time, field_ref, many_ref, few_ref, weights_ref, local_ref,
    part_ref, window, short,
):
    here = lax.axis_index("series")
    many_at = jnp.where(
        here == 0, 0, jnp.where(here == 1, 368, jnp.where(here == 2, 48, 320))
    )
    blocks = [
        (EDGE, jnp.where(here == 0, field_ref[...], 0.0)),
        (many_at, many_ref[...].astype(jnp.float32)),
        (jnp.where(here == 3, 240, 128), few_ref[...].astype(jnp.float32)),
    ]
    product = lag_product(blocks, weights_ref, window, short, last_time)
    part_ref[...] = data_weight * local_ref[...] + scale * product


def halo(here, field, many_ref, few_ref=None):
    rows = field.shape[0]
    late = jnp.logical_or(here == 0, here == 3)
    many = jnp.where(late, field[rows - MANY :], field[:MANY])
    many_ref[...] = many.astype(many_ref.dtype)
    if few_ref is not None:
        few = jnp.where(here == 2, field[rows - FEW :], field[:FEW])
        few_ref[...] = few.astype(few_ref.dtype)


def start_kernel(field_ref, low_ref, many_ref, few_ref):
    field = field_ref[...]
    low_ref[...] = field.astype(jnp.bfloat16)
    halo(lax.axis_index("series"), field, many_ref, few_ref)


def sum_kernel(
    scale, own_ref, first_ref, third_ref, second_ref, field_ref,
    total_ref, low_ref, *halo_refs,
):
    here = lax.axis_index("series")
    total = (own_ref[...] + second_ref[...]) + (first_ref[...] + third_ref[...])
    total = total + scale * field_ref[...]
    total_ref[...] = total
    low_ref[...] = total.astype(jnp.bfloat16)
    halo(here, total, *halo_refs)


def place_sums(sums, first, rank):
    lane = lax.broadcasted_iota(jnp.int32, (1, rank), 1)
    packed = jnp.zeros((1, rank), jnp.float32)
    for number, value in enumerate(sums):
        packed = jnp.where(lane == first + number, value, packed)
    return packed


def inner(left, right):
    return jnp.sum(jnp.sum(left * right, axis=0, keepdims=True), axis=1, keepdims=True)


def products_kernel(share, squares_ref, zero_ref, one_ref, two_ref, packed_ref):
    zero, one, two = zero_ref[...], one_ref[...], two_ref[...]
    sums = [
        inner(zero, zero),
        inner(zero, one),
        inner(zero, two),
        inner(one, one),
        inner(one, two),
        inner(two, two),
    ]
    squares = jnp.sum(squares_ref[...], axis=1, keepdims=True)
    packed = share * place_sums(sums, 0, zero.shape[1])
    packed = packed + place_sums([data_weight * squares], len(sums), zero.shape[1])
    packed_ref[...] = jnp.broadcast_to(packed, packed_ref.shape)


def moments_kernel(
    last_time, packed_ref, two_ref, many_ref,
    weights_ref, spread_ref, window, short,
):
    two = two_ref[...]
    here = lax.axis_index("series")
    many_at = jnp.where(here == 0, 0, jnp.where(here == 2, 48, 128))
    blocks = [
        (EDGE, jnp.where(here == 1, two, 0.0)),
        (many_at, jnp.where(here == 1, 0.0, 2.0 * many_ref[...].astype(jnp.float32))),
    ]
    product = lag_product(blocks, weights_ref, window, short, last_time)
    quadratic = penalty_weight * inner(two, product)
    packed = packed_ref[0:1, :] + place_sums([quadratic], 6, two.shape[1])
    spread_ref[...] = jnp.broadcast_to(packed[None], spread_ref.shape)


def update_kernel(
    gathered_ref, start_ref, zero_ref, one_ref, two_ref, values_ref, factors_ref,
    final_ref, misfit_ref,
):
    total = jnp.sum(gathered_ref[...], axis=0)
    lane = lax.broadcasted_iota(jnp.int32, total.shape, 1)

    def pick(number):
        return jnp.sum(jnp.where(lane == number, total, 0.0), axis=1, keepdims=True)

    m00, m01, m02, m11, m12, m22, m23 = [pick(number) for number in range(7)]
    m23 = m23 + ridge_weight * m22
    alpha0 = m00 / m01
    norm1 = m00 - 2.0 * alpha0 * m01 + alpha0 * alpha0 * m11
    g0 = 1.0 + norm1 / m00
    curvature1 = g0 * g0 * m01 - g0 * alpha0 * (m02 + m11) + alpha0 * alpha0 * m12
    alpha1 = norm1 / curvature1
    a = -(alpha0 + alpha1 * g0)
    b = alpha0 * alpha1
    norm2 = m00 + a * a * m11 + b * b * m22 + 2.0 * (a * m01 + b * m02 + a * b * m12)
    beta1 = norm2 / norm1
    c = 1.0 + beta1 * g0
    d = a - beta1 * alpha0
    curvature2 = (
        c * c * m01
        + c * d * (m02 + m11)
        + 2.0 * c * b * m12
        + d * d * m12
        + 2.0 * d * b * m22
        + b * b * m23
    )
    alpha2 = norm2 / curvature2
    k0 = alpha0 + alpha1 * g0 + alpha2 * c
    k1 = alpha2 * d - alpha1 * alpha0
    k2 = alpha2 * b
    final = start_ref[...] + (k0 * zero_ref[...] + k1 * one_ref[...] + k2 * two_ref[...])
    final_ref[...] = final
    low = final.astype(jnp.bfloat16)
    lanes = misfit_ref.shape[2]
    for first in range(0, values_ref.shape[1], 2 * lanes):
        columns = slice(first, first + 2 * lanes)
        fitted = against(low, factors_ref[columns, :])
        block = (values_ref[:, columns].astype(jnp.float32) - fitted).astype(jnp.bfloat16)
        misfit_ref[first // lanes] = block[:, :lanes]
        misfit_ref[first // lanes + 1] = block[:, lanes:]


def on_device(series_values, observed, series_factors, time_factors, lag_weights):
    rows, rank = time_factors.shape
    n_tm = lax.axis_size("tm")
    n_series = lax.axis_size("series")
    everyone = n_tm * n_series
    last_time = n_tm * rows
    field_shape = jax.ShapeDtypeStruct((rows, rank), jnp.float32)
    many_shape = jax.ShapeDtypeStruct((MANY, rank), jnp.bfloat16)
    few_shape = jax.ShapeDtypeStruct((FEW, rank), jnp.bfloat16)
    halo_shapes = (many_shape, few_shape)
    low_shape = jax.ShapeDtypeStruct((rows, rank), jnp.bfloat16)
    lag_scratch = [
        pltpu.VMEM((2 * EDGE + rows, rank), jnp.float32),
        pltpu.VMEM((rows + SHORT, rank), jnp.float32),
    ]

    def route(steps):
        pairs = []
        for column, step in enumerate(steps):
            if step is None:
                continue
            for source in range(n_tm):
                target = source + step
                if 0 <= target < n_tm:
                    pairs.append((source * n_series + column, target * n_series + column))
        return pairs

    many_route = route([3, -3, 2, -2])
    few_route = route([None, None, 1, -1])
    last_route = route([3, None, 2, 1])
    both = ("tm", "series")

    def fetch(many, few):
        few = lax.ppermute(few, both, few_route)
        return lax.ppermute(many, both, many_route), few

    def penalty(scale, field, many, few, local):
        return pl.pallas_call(
            functools.partial(penalty_kernel, scale, last_time),
            out_shape=field_shape,
            in_specs=[VMEM] * 5,
            out_specs=VMEM,
            scratch_shapes=lag_scratch,
            compiler_params=SMALL,
        )(field, many, few, lag_weights, local)

    def series_sum(scale, part, field, out_halos):
        def moved(distance):
            pairs = [(i, (i + distance) % n_series) for i in range(n_series)]
            return lax.ppermute(part, "series", pairs)

        first, third = moved(1), moved(3)
        second = moved(2)
        return pl.pallas_call(
            functools.partial(sum_kernel, scale),
            out_shape=(field_shape, low_shape) + out_halos,
            in_specs=[VMEM] * 5,
            out_specs=(VMEM,) * (2 + len(out_halos)),
            compiler_params=SMALL,
        )(part, first, third, second, field)

    seen = observed == 1

    def fit(low):
        return jnp.where(seen, against(low, series_factors), 0.0)

    def back(rows_here):
        return jnp.dot(rows_here, series_factors, preferred_element_type=jnp.float32)

    low, many, few = pl.pallas_call(
        start_kernel,
        out_shape=(low_shape, many_shape, few_shape),
        in_specs=[VMEM],
        out_specs=(VMEM,) * 3,
        compiler_params=SMALL,
    )(time_factors)
    many, few = fetch(many, few)
    kept = jnp.where(seen, series_values, jnp.zeros((), jnp.bfloat16))
    local = back(kept) - back(fit(low).astype(jnp.bfloat16))
    part = penalty(-penalty_weight, time_factors, many, few, local)
    power0, low, many, few = series_sum(-ridge_weight, part, time_factors, halo_shapes)

    def image(field, low, many, few, out_halos):
        many, few = fetch(many, few)
        local = back(fit(low).astype(jnp.bfloat16))
        part = penalty(penalty_weight, field, many, few, local)
        return series_sum(ridge_weight, part, field, out_halos)

    power1, low, many, few = image(power0, low, many, few, halo_shapes)
    power2, low, many = image(power1, low, many, few, (many_shape,))
    many = lax.ppermute(many, both, last_route)
    fitted = fit(low)
    squares = jnp.sum(fitted * fitted, axis=0, keepdims=True)
    packed = pl.pallas_call(
        functools.partial(products_kernel, 1.0 / n_series),
        out_shape=jax.ShapeDtypeStruct((8, rank), jnp.float32),
        in_specs=[VMEM] * 4,
        out_specs=VMEM,
        compiler_params=SMALL,
    )(squares, power0, power1, power2)
    spread = pl.pallas_call(
        functools.partial(moments_kernel, last_time),
        out_shape=jax.ShapeDtypeStruct((everyone, 1, rank), jnp.float32),
        in_specs=[VMEM] * 4,
        out_specs=VMEM,
        scratch_shapes=lag_scratch,
        compiler_params=SMALL,
    )(packed, power2, many, lag_weights)
    gathered = lax.all_to_all(spread, both, split_axis=0, concat_axis=0, tiled=True)
    final, misfit = pl.pallas_call(
        update_kernel,
        out_shape=(field_shape, jax.ShapeDtypeStruct((n_tm, rows, rank), jnp.bfloat16)),
        in_specs=[VMEM] * 7,
        out_specs=(VMEM, VMEM),
        compiler_params=SMALL,
    )(gathered, time_factors, power0, power1, power2, series_values, series_factors)
    misfit = lax.all_to_all(misfit, "tm", split_axis=0, concat_axis=0, tiled=True)
    return final, misfit.reshape(n_tm * rows, rank)


def solution(mesh):
    placed = (P("tm", "series"), P("tm", "series"), P("series", None), P("tm", None), P())
    return jax.shard_map(
        on_device,
        mesh=mesh,
        in_specs=placed,
        out_specs=(P("tm", None), P(None, ("series", "tm"))),
        check_vma=False,
    )
```

```python
import functools

import jax
import jax.numpy as jnp
from jax import lax
from jax.experimental import pallas as pl
from jax.experimental.pallas import tpu as pltpu
from jax.sharding import PartitionSpec as P

SHORT = 24
SEASON = 168
LAGS = list(range(1, SHORT + 1)) + [SEASON]
MANY = 48
EDGE = SEASON + 8
data_weight = 2.0
penalty_weight = 0.5
ridge_weight = 0.2

VMEM = pl.BlockSpec(memory_space=pltpu.VMEM)
SMALL = pltpu.CompilerParams(vmem_limit_bytes=2 << 20)


def against(left_rows, factors):
    return lax.dot_general(
        left_rows, factors, (((1,), (1,)), ((), ())), preferred_element_type=jnp.float32
    )


def lag_product(blocks, weights_ref, window, short, last_time):
    rank = weights_ref.shape[1]
    rows = window.shape[0] - 2 * EDGE
    first_time = lax.axis_index("tm") * rows
    window[...] = jnp.zeros_like(window)
    for start, block in blocks:
        if not isinstance(start, int):
            start = pl.multiple_of(start, 8)
        window[pl.ds(start, block.shape[0]), :] = block

    def weight(number):
        return weights_ref[number : number + 1, :]

    def lagged(start, count):
        base = EDGE + start
        result = window[base : base + count, :]
        for number, lag in enumerate(LAGS):
            result = result - weight(number) * window[base - lag : base - lag + count, :]
        stamp = first_time + start + lax.broadcasted_iota(jnp.int32, (count, rank), 0)
        return jnp.where(stamp < last_time, result, 0.0)

    short[...] = lagged(0, rows + SHORT)
    result = short[0:rows, :] - weight(SHORT) * lagged(SEASON, rows)
    for number in range(SHORT):
        lag = LAGS[number]
        result = result - weight(number) * short[lag : lag + rows, :]
    return result


def penalty_kernel(
    scale, last_time, field_ref, many_ref, few_ref, weights_ref, local_ref,
    part_ref, window, short,
):
    here = lax.axis_index("series")
    many_at = jnp.where(
        here == 0, 0, jnp.where(here == 1, 368, jnp.where(here == 2, 48, 320))
    )
    blocks = [
        (EDGE, jnp.where(here == 0, field_ref[...], 0.0)),
        (many_at, many_ref[...].astype(jnp.float32)),
        (jnp.where(here == 2, 240, 128), few_ref[...].astype(jnp.float32)),
    ]
    product = lag_product(blocks, weights_ref, window, short, last_time)
    part_ref[...] = data_weight * local_ref[...] + scale * product


def halo_rows(field):
    here = lax.axis_index("series")
    late = jnp.logical_or(here == 0, here == 3)
    rows = field.shape[0]
    return jnp.where(late, field[rows - MANY :], field[:MANY]).astype(jnp.bfloat16)


def start_kernel(field_ref, low_ref, halo_ref):
    field = field_ref[...]
    low_ref[...] = field.astype(jnp.bfloat16)
    halo_ref[...] = halo_rows(field)


def sum_kernel(
    scale, own_ref, first_ref, third_ref, second_ref, field_ref,
    total_ref, low_ref, halo_ref,
):
    total = (own_ref[...] + second_ref[...]) + (first_ref[...] + third_ref[...])
    total = total + scale * field_ref[...]
    total_ref[...] = total
    low_ref[...] = total.astype(jnp.bfloat16)
    halo_ref[...] = halo_rows(total)


def place_sums(sums, first, rank):
    lane = lax.broadcasted_iota(jnp.int32, (1, rank), 1)
    packed = jnp.zeros((1, rank), jnp.float32)
    for number, value in enumerate(sums):
        packed = jnp.where(lane == first + number, value, packed)
    return packed


def inner(left, right):
    return jnp.sum(jnp.sum(left * right, axis=0, keepdims=True), axis=1, keepdims=True)


def products_kernel(share, squares_ref, zero_ref, one_ref, two_ref, packed_ref):
    zero, one, two = zero_ref[...], one_ref[...], two_ref[...]
    sums = [
        inner(zero, zero),
        inner(zero, one),
        inner(zero, two),
        inner(one, one),
        inner(one, two),
        inner(two, two),
    ]
    squares = jnp.sum(squares_ref[...], axis=1, keepdims=True)
    packed = share * place_sums(sums, 0, zero.shape[1])
    packed = packed + place_sums([data_weight * squares], len(sums), zero.shape[1])
    packed_ref[...] = jnp.broadcast_to(packed, packed_ref.shape)


def moments_kernel(
    last_time, packed_ref, two_ref, many_ref,
    weights_ref, spread_ref, window, short,
):
    two = two_ref[...]
    here = lax.axis_index("series")
    many_at = jnp.where(here == 0, 0, jnp.where(here == 2, 48, 128))
    blocks = [
        (EDGE, jnp.where(here == 1, two, 0.0)),
        (many_at, jnp.where(here == 1, 0.0, 2.0 * many_ref[...].astype(jnp.float32))),
    ]
    product = lag_product(blocks, weights_ref, window, short, last_time)
    quadratic = penalty_weight * inner(two, product)
    packed = packed_ref[0:1, :] + place_sums([quadratic], 6, two.shape[1])
    spread_ref[...] = jnp.broadcast_to(packed[None], spread_ref.shape)


def update_kernel(
    gathered_ref, start_ref, zero_ref, one_ref, two_ref, values_ref, factors_ref,
    final_ref, misfit_ref,
):
    total = jnp.sum(gathered_ref[...], axis=0)
    lane = lax.broadcasted_iota(jnp.int32, total.shape, 1)

    def pick(number):
        return jnp.sum(jnp.where(lane == number, total, 0.0), axis=1, keepdims=True)

    m00, m01, m02, m11, m12, m22, m23 = [pick(number) for number in range(7)]
    m23 = m23 + ridge_weight * m22
    alpha0 = m00 / m01
    norm1 = m00 - 2.0 * alpha0 * m01 + alpha0 * alpha0 * m11
    g0 = 1.0 + norm1 / m00
    curvature1 = g0 * g0 * m01 - g0 * alpha0 * (m02 + m11) + alpha0 * alpha0 * m12
    alpha1 = norm1 / curvature1
    a = -(alpha0 + alpha1 * g0)
    b = alpha0 * alpha1
    norm2 = m00 + a * a * m11 + b * b * m22 + 2.0 * (a * m01 + b * m02 + a * b * m12)
    beta1 = norm2 / norm1
    c = 1.0 + beta1 * g0
    d = a - beta1 * alpha0
    curvature2 = (
        c * c * m01
        + c * d * (m02 + m11)
        + 2.0 * c * b * m12
        + d * d * m12
        + 2.0 * d * b * m22
        + b * b * m23
    )
    alpha2 = norm2 / curvature2
    k0 = alpha0 + alpha1 * g0 + alpha2 * c
    k1 = alpha2 * d - alpha1 * alpha0
    k2 = alpha2 * b
    final = start_ref[...] + (k0 * zero_ref[...] + k1 * one_ref[...] + k2 * two_ref[...])
    final_ref[...] = final
    low = final.astype(jnp.bfloat16)
    lanes = misfit_ref.shape[2]
    for first in range(0, values_ref.shape[1], 2 * lanes):
        columns = slice(first, first + 2 * lanes)
        fitted = against(low, factors_ref[columns, :])
        block = (values_ref[:, columns].astype(jnp.float32) - fitted).astype(jnp.bfloat16)
        misfit_ref[first // lanes] = block[:, :lanes]
        misfit_ref[first // lanes + 1] = block[:, lanes:]


def on_device(series_values, observed, series_factors, time_factors, lag_weights):
    rows, rank = time_factors.shape
    n_tm = lax.axis_size("tm")
    n_series = lax.axis_size("series")
    everyone = n_tm * n_series
    last_time = n_tm * rows
    field_shape = jax.ShapeDtypeStruct((rows, rank), jnp.float32)
    halo_shape = jax.ShapeDtypeStruct((MANY, rank), jnp.bfloat16)
    low_shape = jax.ShapeDtypeStruct((rows, rank), jnp.bfloat16)
    lag_scratch = [
        pltpu.VMEM((2 * EDGE + rows, rank), jnp.float32),
        pltpu.VMEM((rows + SHORT, rank), jnp.float32),
    ]

    def route(steps):
        pairs = []
        for column, step in enumerate(steps):
            if step is None:
                continue
            for source in range(n_tm):
                target = source + step
                if 0 <= target < n_tm:
                    pairs.append((source * n_series + column, target * n_series + column))
        return pairs

    many_route = route([3, -3, 2, -2])
    few_route = route([None, None, -1, 1])
    last_route = route([3, None, 2, 1])
    both = ("tm", "series")

    def fetch(halo):
        return lax.ppermute(halo, both, many_route), lax.ppermute(halo, both, few_route)

    def penalty(scale, field, many, few, local):
        return pl.pallas_call(
            functools.partial(penalty_kernel, scale, last_time),
            out_shape=field_shape,
            in_specs=[VMEM] * 5,
            out_specs=VMEM,
            scratch_shapes=lag_scratch,
            compiler_params=SMALL,
        )(field, many, few, lag_weights, local)

    def series_sum(scale, part, field):
        def moved(distance):
            pairs = [(i, (i + distance) % n_series) for i in range(n_series)]
            return lax.ppermute(part, "series", pairs)

        first, third = moved(1), moved(3)
        second = moved(2)
        return pl.pallas_call(
            functools.partial(sum_kernel, scale),
            out_shape=(field_shape, low_shape, halo_shape),
            in_specs=[VMEM] * 5,
            out_specs=(VMEM,) * 3,
            compiler_params=SMALL,
        )(part, first, third, second, field)

    seen = observed == 1

    def fit(low):
        return jnp.where(seen, against(low, series_factors), 0.0)

    def back(rows_here):
        return jnp.dot(rows_here, series_factors, preferred_element_type=jnp.float32)

    low, halo = pl.pallas_call(
        start_kernel,
        out_shape=(low_shape, halo_shape),
        in_specs=[VMEM],
        out_specs=(VMEM,) * 2,
        compiler_params=SMALL,
    )(time_factors)
    many, few = fetch(halo)
    kept = jnp.where(seen, series_values, jnp.zeros((), jnp.bfloat16))
    local = back(kept) - back(fit(low).astype(jnp.bfloat16))
    part = penalty(-penalty_weight, time_factors, many, few, local)
    power0, low, halo = series_sum(-ridge_weight, part, time_factors)

    def image(field, low, halo):
        many, few = fetch(halo)
        local = back(fit(low).astype(jnp.bfloat16))
        part = penalty(penalty_weight, field, many, few, local)
        return series_sum(ridge_weight, part, field)

    power1, low, halo = image(power0, low, halo)
    power2, low, halo = image(power1, low, halo)
    many = lax.ppermute(halo, both, last_route)
    fitted = fit(low)
    squares = jnp.sum(fitted * fitted, axis=0, keepdims=True)
    packed = pl.pallas_call(
        functools.partial(products_kernel, 1.0 / n_series),
        out_shape=jax.ShapeDtypeStruct((8, rank), jnp.float32),
        in_specs=[VMEM] * 4,
        out_specs=VMEM,
        compiler_params=SMALL,
    )(squares, power0, power1, power2)
    spread = pl.pallas_call(
        functools.partial(moments_kernel, last_time),
        out_shape=jax.ShapeDtypeStruct((everyone, 1, rank), jnp.float32),
        in_specs=[VMEM] * 4,
        out_specs=VMEM,
        scratch_shapes=lag_scratch,
        compiler_params=SMALL,
    )(packed, power2, many, lag_weights)
    gathered = lax.all_to_all(spread, both, split_axis=0, concat_axis=0, tiled=True)
    final, misfit = pl.pallas_call(
        update_kernel,
        out_shape=(field_shape, jax.ShapeDtypeStruct((n_tm, rows, rank), jnp.bfloat16)),
        in_specs=[VMEM] * 7,
        out_specs=(VMEM, VMEM),
        compiler_params=SMALL,
    )(gathered, time_factors, power0, power1, power2, series_values, series_factors)
    misfit = lax.all_to_all(misfit, "tm", split_axis=0, concat_axis=0, tiled=True)
    return final, misfit.reshape(n_tm * rows, rank)


def solution(mesh):
    placed = (P("tm", "series"), P("tm", "series"), P("series", None), P("tm", None), P())
    return jax.shard_map(
        on_device,
        mesh=mesh,
        in_specs=placed,
        out_specs=(P("tm", None), P(None, ("series", "tm"))),
        check_vma=False,
    )
```

```python
import functools

import jax
import jax.numpy as jnp
from jax import lax
from jax.experimental import pallas as pl
from jax.experimental.pallas import tpu as pltpu
from jax.sharding import PartitionSpec as P

SHORT = 24
SEASON = 168
LAGS = list(range(1, SHORT + 1)) + [SEASON]
MANY = 48
EDGE = SEASON + 8
data_weight = 2.0
penalty_weight = 0.5
ridge_weight = 0.2

VMEM = pl.BlockSpec(memory_space=pltpu.VMEM)
SMALL = pltpu.CompilerParams(vmem_limit_bytes=2 << 20)


def against(left_rows, factors):
    return lax.dot_general(
        left_rows, factors, (((1,), (1,)), ((), ())), preferred_element_type=jnp.float32
    )


def lag_product(blocks, weights_ref, window, short, last_time):
    rank = weights_ref.shape[1]
    rows = window.shape[0] - 2 * EDGE
    first_time = lax.axis_index("tm") * rows
    window[...] = jnp.zeros_like(window)
    for start, block in blocks:
        if not isinstance(start, int):
            start = pl.multiple_of(start, 8)
        window[pl.ds(start, block.shape[0]), :] = block

    def weight(number):
        return weights_ref[number : number + 1, :]

    def lagged(start, count):
        base = EDGE + start
        result = window[base : base + count, :]
        for number, lag in enumerate(LAGS):
            result = result - weight(number) * window[base - lag : base - lag + count, :]
        stamp = first_time + start + lax.broadcasted_iota(jnp.int32, (count, rank), 0)
        return jnp.where(stamp < last_time, result, 0.0)

    short[...] = lagged(0, rows + SHORT)
    result = short[0:rows, :] - weight(SHORT) * lagged(SEASON, rows)
    for number in range(SHORT):
        lag = LAGS[number]
        result = result - weight(number) * short[lag : lag + rows, :]
    return result


def penalty_kernel(
    scale, last_time, field_ref, few_ref, many_ref, weights_ref, local_ref,
    part_ref, window, short,
):
    here = lax.axis_index("series")
    many_at = jnp.where(
        here == 0, 0, jnp.where(here == 1, 368, jnp.where(here == 2, 48, 320))
    )
    blocks = [
        (EDGE, jnp.where(here == 0, field_ref[...], 0.0)),
        (many_at, halo_rows(many_ref[...].astype(jnp.float32))),
        (jnp.where(here == 2, 240, 128), halo_rows(few_ref[...].astype(jnp.float32))),
    ]
    product = lag_product(blocks, weights_ref, window, short, last_time)
    part_ref[...] = data_weight * local_ref[...] + scale * product


def halo_rows(field):
    here = lax.axis_index("series")
    late = jnp.logical_or(here == 0, here == 3)
    rows = field.shape[0]
    if rows == MANY:
        return field
    return jnp.where(late, field[rows - MANY :], field[:MANY])


def sum_kernel(
    scale, own_ref, first_ref, third_ref, second_ref, field_ref,
    total_ref, low_ref, halo_ref,
):
    total = (own_ref[...] + second_ref[...]) + (first_ref[...] + third_ref[...])
    total = total + scale * field_ref[...]
    total_ref[...] = total
    low_ref[...] = total.astype(jnp.bfloat16)
    halo_ref[...] = halo_rows(total).astype(jnp.bfloat16)


def place_sums(sums, first, rank):
    lane = lax.broadcasted_iota(jnp.int32, (1, rank), 1)
    packed = jnp.zeros((1, rank), jnp.float32)
    for number, value in enumerate(sums):
        packed = jnp.where(lane == first + number, value, packed)
    return packed


def inner(left, right):
    return jnp.sum(jnp.sum(left * right, axis=0, keepdims=True), axis=1, keepdims=True)


def products_kernel(share, squares_ref, zero_ref, one_ref, two_ref, packed_ref):
    zero, one, two = zero_ref[...], one_ref[...], two_ref[...]
    sums = [
        inner(zero, zero),
        inner(zero, one),
        inner(zero, two),
        inner(one, one),
        inner(one, two),
        inner(two, two),
    ]
    squares = jnp.sum(squares_ref[...], axis=1, keepdims=True)
    packed = share * place_sums(sums, 0, zero.shape[1])
    packed = packed + place_sums([data_weight * squares], len(sums), zero.shape[1])
    packed_ref[...] = jnp.broadcast_to(packed, packed_ref.shape)


def moments_kernel(
    last_time, packed_ref, two_ref, many_ref,
    weights_ref, spread_ref, window, short,
):
    two = two_ref[...]
    here = lax.axis_index("series")
    many_at = jnp.where(here == 0, 0, jnp.where(here == 2, 48, 128))
    blocks = [
        (EDGE, jnp.where(here == 1, two, 0.0)),
        (many_at, jnp.where(here == 1, 0.0, 2.0 * many_ref[...].astype(jnp.float32))),
    ]
    product = lag_product(blocks, weights_ref, window, short, last_time)
    quadratic = penalty_weight * inner(two, product)
    packed = packed_ref[0:1, :] + place_sums([quadratic], 6, two.shape[1])
    spread_ref[...] = jnp.broadcast_to(packed[None], spread_ref.shape)


def update_kernel(
    gathered_ref, start_ref, zero_ref, one_ref, two_ref, values_ref, factors_ref,
    final_ref, misfit_ref,
):
    total = gathered_ref[...]
    while total.shape[0] > 1:
        half = total.shape[0] // 2
        total = total[:half] + total[half:]
    total = total[0]
    lane = lax.broadcasted_iota(jnp.int32, total.shape, 1)

    def pick(number):
        return jnp.sum(jnp.where(lane == number, total, 0.0), axis=1, keepdims=True)

    m00, m01, m02, m11, m12, m22, m23 = [pick(number) for number in range(7)]
    m23 = m23 + ridge_weight * m22
    alpha0 = m00 / m01
    norm1 = m00 - 2.0 * alpha0 * m01 + alpha0 * alpha0 * m11
    g0 = 1.0 + norm1 / m00
    curvature1 = g0 * g0 * m01 - g0 * alpha0 * (m02 + m11) + alpha0 * alpha0 * m12
    alpha1 = norm1 / curvature1
    a = -(alpha0 + alpha1 * g0)
    b = alpha0 * alpha1
    norm2 = m00 + a * a * m11 + b * b * m22 + 2.0 * (a * m01 + b * m02 + a * b * m12)
    beta1 = norm2 / norm1
    c = 1.0 + beta1 * g0
    d = a - beta1 * alpha0
    curvature2 = (
        c * c * m01
        + c * d * (m02 + m11)
        + 2.0 * c * b * m12
        + d * d * m12
        + 2.0 * d * b * m22
        + b * b * m23
    )
    alpha2 = norm2 / curvature2
    k0 = alpha0 + alpha1 * g0 + alpha2 * c
    k1 = alpha2 * d - alpha1 * alpha0
    k2 = alpha2 * b
    final = start_ref[...] + (k0 * zero_ref[...] + k1 * one_ref[...] + k2 * two_ref[...])
    final_ref[...] = final
    low = final.astype(jnp.bfloat16)
    lanes = misfit_ref.shape[2]
    for first in range(0, values_ref.shape[1], 2 * lanes):
        columns = slice(first, first + 2 * lanes)
        fitted = against(low, factors_ref[columns, :])
        block = (values_ref[:, columns].astype(jnp.float32) - fitted).astype(jnp.bfloat16)
        misfit_ref[first // lanes] = block[:, :lanes]
        misfit_ref[first // lanes + 1] = block[:, lanes:]


def on_device(series_values, observed, series_factors, time_factors, lag_weights):
    rows, rank = time_factors.shape
    n_tm = lax.axis_size("tm")
    n_series = lax.axis_size("series")
    everyone = n_tm * n_series
    last_time = n_tm * rows
    field_shape = jax.ShapeDtypeStruct((rows, rank), jnp.float32)
    halo_shape = jax.ShapeDtypeStruct((MANY, rank), jnp.bfloat16)
    low_shape = jax.ShapeDtypeStruct((rows, rank), jnp.bfloat16)
    lag_scratch = [
        pltpu.VMEM((2 * EDGE + rows, rank), jnp.float32),
        pltpu.VMEM((rows + SHORT, rank), jnp.float32),
    ]

    def route(steps):
        pairs = []
        for column, step in enumerate(steps):
            if step is None:
                continue
            for source in range(n_tm):
                target = source + step
                if 0 <= target < n_tm:
                    pairs.append((source * n_series + column, target * n_series + column))
        return pairs

    many_route = route([3, -3, 2, -2])
    few_route = route([None, None, -1, 1])
    last_route = route([3, None, 2, 1])
    both = ("tm", "series")

    def fetch(halo):
        return lax.ppermute(halo, both, many_route), lax.ppermute(halo, both, few_route)

    def penalty(scale, field, many, few, local):
        return pl.pallas_call(
            functools.partial(penalty_kernel, scale, last_time),
            out_shape=field_shape,
            in_specs=[VMEM] * 5,
            out_specs=VMEM,
            scratch_shapes=lag_scratch,
            compiler_params=SMALL,
        )(field, few, many, lag_weights, local)

    def series_sum(scale, part, field):
        def moved(distance):
            pairs = [(i, (i + distance) % n_series) for i in range(n_series)]
            return lax.ppermute(part, "series", pairs)

        first, third = moved(1), moved(3)
        second = moved(2)
        return pl.pallas_call(
            functools.partial(sum_kernel, scale),
            out_shape=(field_shape, low_shape, halo_shape),
            in_specs=[VMEM] * 5,
            out_specs=(VMEM,) * 3,
            compiler_params=SMALL,
        )(part, first, third, second, field)

    seen = observed == 1

    def fit(low):
        return jnp.where(seen, against(low, series_factors), 0.0)

    def back(rows_here):
        return jnp.dot(rows_here, series_factors, preferred_element_type=jnp.float32)

    low = time_factors.astype(jnp.bfloat16)
    many, few = fetch(time_factors)
    kept = jnp.where(seen, series_values, jnp.zeros((), jnp.bfloat16))
    local = back(kept) - back(fit(low).astype(jnp.bfloat16))
    part = penalty(-penalty_weight, time_factors, many, few, local)
    power0, low, halo = series_sum(-ridge_weight, part, time_factors)

    def image(field, low, halo):
        many, few = fetch(halo)
        local = back(fit(low).astype(jnp.bfloat16))
        part = penalty(penalty_weight, field, many, few, local)
        return series_sum(ridge_weight, part, field)

    power1, low, halo = image(power0, low, halo)
    power2, low, halo = image(power1, low, halo)
    many = lax.ppermute(halo, both, last_route)
    fitted = fit(low)
    squares = jnp.sum(fitted * fitted, axis=0, keepdims=True)
    packed = pl.pallas_call(
        functools.partial(products_kernel, 1.0 / n_series),
        out_shape=jax.ShapeDtypeStruct((8, rank), jnp.float32),
        in_specs=[VMEM] * 4,
        out_specs=VMEM,
        compiler_params=SMALL,
    )(squares, power0, power1, power2)
    spread = pl.pallas_call(
        functools.partial(moments_kernel, last_time),
        out_shape=jax.ShapeDtypeStruct((everyone, 1, rank), jnp.float32),
        in_specs=[VMEM] * 4,
        out_specs=VMEM,
        scratch_shapes=lag_scratch,
        compiler_params=SMALL,
    )(packed, power2, many, lag_weights)
    gathered = lax.all_to_all(spread, both, split_axis=0, concat_axis=0, tiled=True)
    final, misfit = pl.pallas_call(
        update_kernel,
        out_shape=(field_shape, jax.ShapeDtypeStruct((n_tm, rows, rank), jnp.bfloat16)),
        in_specs=[VMEM] * 7,
        out_specs=(VMEM, VMEM),
        compiler_params=SMALL,
    )(gathered, time_factors, power0, power1, power2, series_values, series_factors)
    misfit = lax.all_to_all(misfit, "tm", split_axis=0, concat_axis=0, tiled=True)
    return final, misfit.reshape(n_tm * rows, rank)


def solution(mesh):
    placed = (P("tm", "series"), P("tm", "series"), P("series", None), P("tm", None), P())
    return jax.shard_map(
        on_device,
        mesh=mesh,
        in_specs=placed,
        out_specs=(P("tm", None), P(None, ("series", "tm"))),
        check_vma=False,
    )
```

```python
import functools

import jax
import jax.numpy as jnp
from jax import lax
from jax.experimental import pallas as pl
from jax.experimental.pallas import tpu as pltpu
from jax.sharding import PartitionSpec as P

SHORT = 24
SEASON = 168
LAGS = list(range(1, SHORT + 1)) + [SEASON]
MANY = 48
EDGE = SEASON + 8
data_weight = 2.0
penalty_weight = 0.5
ridge_weight = 0.2

VMEM = pl.BlockSpec(memory_space=pltpu.VMEM)
SMALL = pltpu.CompilerParams(vmem_limit_bytes=2 << 20)


def against(left_rows, factors):
    return lax.dot_general(
        left_rows, factors, (((1,), (1,)), ((), ())), preferred_element_type=jnp.float32
    )


def lag_product(blocks, weights_ref, window, short, last_time):
    rank = weights_ref.shape[1]
    rows = window.shape[0] - 2 * EDGE
    first_time = lax.axis_index("tm") * rows
    window[...] = jnp.zeros_like(window)
    for start, block in blocks:
        if not isinstance(start, int):
            start = pl.multiple_of(start, 8)
        window[pl.ds(start, block.shape[0]), :] = block

    def weight(number):
        return weights_ref[number : number + 1, :]

    def lagged(start, count):
        base = EDGE + start
        result = window[base : base + count, :]
        for number, lag in enumerate(LAGS):
            result = result - weight(number) * window[base - lag : base - lag + count, :]
        stamp = first_time + start + lax.broadcasted_iota(jnp.int32, (count, rank), 0)
        return jnp.where(stamp < last_time, result, 0.0)

    short[...] = lagged(0, rows + SHORT)
    result = short[0:rows, :] - weight(SHORT) * lagged(SEASON, rows)
    for number in range(SHORT):
        lag = LAGS[number]
        result = result - weight(number) * short[lag : lag + rows, :]
    return result


def penalty_kernel(
    scale, last_time, field_ref, many_ref, few_ref, weights_ref, local_ref,
    part_ref, window, short,
):
    here = lax.axis_index("series")
    many_at = jnp.where(
        here == 0, 0, jnp.where(here == 1, 368, jnp.where(here == 2, 48, 320))
    )
    blocks = [
        (EDGE, jnp.where(here == 0, field_ref[...], 0.0)),
        (many_at, long_rows(here, many_ref[...].astype(jnp.float32))),
        (jnp.where(here == 3, 240, 128), short_rows(here, few_ref[...].astype(jnp.float32))),
    ]
    product = lag_product(blocks, weights_ref, window, short, last_time)
    part_ref[...] = data_weight * local_ref[...] + scale * product


def rows_for(late, field):
    rows = field.shape[0]
    if rows == MANY:
        return field
    return jnp.where(late, field[rows - MANY :], field[:MANY])


def long_rows(here, field):
    return rows_for(jnp.logical_or(here == 0, here == 3), field)


def short_rows(here, field):
    return rows_for(here == 2, field)


def sum_kernel(
    scale, own_ref, first_ref, third_ref, second_ref, field_ref,
    total_ref, low_ref, *halo_refs,
):
    here = lax.axis_index("series")
    total = (own_ref[...] + second_ref[...]) + (first_ref[...] + third_ref[...])
    total = total + scale * field_ref[...]
    total_ref[...] = total
    low_ref[...] = total.astype(jnp.bfloat16)
    halo_refs[0][...] = long_rows(here, total).astype(jnp.bfloat16)
    if len(halo_refs) > 1:
        halo_refs[1][...] = short_rows(here, total).astype(jnp.bfloat16)


def place_sums(sums, first, rank):
    lane = lax.broadcasted_iota(jnp.int32, (1, rank), 1)
    packed = jnp.zeros((1, rank), jnp.float32)
    for number, value in enumerate(sums):
        packed = jnp.where(lane == first + number, value, packed)
    return packed


def inner(left, right):
    return jnp.sum(jnp.sum(left * right, axis=0, keepdims=True), axis=1, keepdims=True)


def products_kernel(share, squares_ref, zero_ref, one_ref, two_ref, packed_ref):
    zero, one, two = zero_ref[...], one_ref[...], two_ref[...]
    sums = [
        inner(zero, zero),
        inner(zero, one),
        inner(zero, two),
        inner(one, one),
        inner(one, two),
        inner(two, two),
    ]
    squares = jnp.sum(squares_ref[...], axis=1, keepdims=True)
    packed = share * place_sums(sums, 0, zero.shape[1])
    packed = packed + place_sums([data_weight * squares], len(sums), zero.shape[1])
    packed_ref[...] = jnp.broadcast_to(packed, packed_ref.shape)


def moments_kernel(
    last_time, packed_ref, two_ref, many_ref,
    weights_ref, spread_ref, window, short,
):
    two = two_ref[...]
    here = lax.axis_index("series")
    many_at = jnp.where(here == 0, 0, jnp.where(here == 2, 48, 128))
    blocks = [
        (EDGE, jnp.where(here == 1, two, 0.0)),
        (many_at, jnp.where(here == 1, 0.0, 2.0 * many_ref[...].astype(jnp.float32))),
    ]
    product = lag_product(blocks, weights_ref, window, short, last_time)
    quadratic = penalty_weight * inner(two, product)
    packed = packed_ref[0:1, :] + place_sums([quadratic], 6, two.shape[1])
    spread_ref[...] = jnp.broadcast_to(packed[None], spread_ref.shape)


def update_kernel(
    gathered_ref, start_ref, zero_ref, one_ref, two_ref, values_ref, factors_ref,
    final_ref, misfit_ref,
):
    total = gathered_ref[...]
    while total.shape[0] > 1:
        half = total.shape[0] // 2
        total = total[:half] + total[half:]
    total = total[0]
    lane = lax.broadcasted_iota(jnp.int32, total.shape, 1)

    def pick(number):
        return jnp.sum(jnp.where(lane == number, total, 0.0), axis=1, keepdims=True)

    m00, m01, m02, m11, m12, m22, m23 = [pick(number) for number in range(7)]
    m23 = m23 + ridge_weight * m22
    alpha0 = m00 / m01
    norm1 = m00 - 2.0 * alpha0 * m01 + alpha0 * alpha0 * m11
    g0 = 1.0 + norm1 / m00
    curvature1 = g0 * g0 * m01 - g0 * alpha0 * (m02 + m11) + alpha0 * alpha0 * m12
    alpha1 = norm1 / curvature1
    a = -(alpha0 + alpha1 * g0)
    b = alpha0 * alpha1
    norm2 = m00 + a * a * m11 + b * b * m22 + 2.0 * (a * m01 + b * m02 + a * b * m12)
    beta1 = norm2 / norm1
    c = 1.0 + beta1 * g0
    d = a - beta1 * alpha0
    curvature2 = (
        c * c * m01
        + c * d * (m02 + m11)
        + 2.0 * c * b * m12
        + d * d * m12
        + 2.0 * d * b * m22
        + b * b * m23
    )
    alpha2 = norm2 / curvature2
    k0 = alpha0 + alpha1 * g0 + alpha2 * c
    k1 = alpha2 * d - alpha1 * alpha0
    k2 = alpha2 * b
    final = start_ref[...] + (k0 * zero_ref[...] + k1 * one_ref[...] + k2 * two_ref[...])
    final_ref[...] = final
    low = final.astype(jnp.bfloat16)
    lanes = misfit_ref.shape[2]
    for first in range(0, values_ref.shape[1], 2 * lanes):
        columns = slice(first, first + 2 * lanes)
        fitted = against(low, factors_ref[columns, :])
        block = (values_ref[:, columns].astype(jnp.float32) - fitted).astype(jnp.bfloat16)
        misfit_ref[first // lanes] = block[:, :lanes]
        misfit_ref[first // lanes + 1] = block[:, lanes:]


def on_device(series_values, observed, series_factors, time_factors, lag_weights):
    rows, rank = time_factors.shape
    n_tm = lax.axis_size("tm")
    n_series = lax.axis_size("series")
    everyone = n_tm * n_series
    last_time = n_tm * rows
    field_shape = jax.ShapeDtypeStruct((rows, rank), jnp.float32)
    many_shape = jax.ShapeDtypeStruct((MANY, rank), jnp.bfloat16)
    few_shape = jax.ShapeDtypeStruct((MANY, rank), jnp.bfloat16)
    halo_shapes = (many_shape, few_shape)
    low_shape = jax.ShapeDtypeStruct((rows, rank), jnp.bfloat16)
    lag_scratch = [
        pltpu.VMEM((2 * EDGE + rows, rank), jnp.float32),
        pltpu.VMEM((rows + SHORT, rank), jnp.float32),
    ]

    def route(steps):
        pairs = []
        for column, step in enumerate(steps):
            if step is None:
                continue
            for source in range(n_tm):
                target = source + step
                if 0 <= target < n_tm:
                    pairs.append((source * n_series + column, target * n_series + column))
        return pairs

    many_route = route([3, -3, 2, -2])
    few_route = route([None, None, 1, -1])
    last_route = route([3, None, 2, 1])
    both = ("tm", "series")

    def fetch(many, few):
        few = lax.ppermute(few, both, few_route)
        return lax.ppermute(many, both, many_route), few

    def penalty(scale, field, many, few, local):
        return pl.pallas_call(
            functools.partial(penalty_kernel, scale, last_time),
            out_shape=field_shape,
            in_specs=[VMEM] * 5,
            out_specs=VMEM,
            scratch_shapes=lag_scratch,
            compiler_params=SMALL,
        )(field, many, few, lag_weights, local)

    def series_sum(scale, part, field, out_halos):
        def moved(distance):
            pairs = [(i, (i + distance) % n_series) for i in range(n_series)]
            return lax.ppermute(part, "series", pairs)

        first, third = moved(1), moved(3)
        second = moved(2)
        return pl.pallas_call(
            functools.partial(sum_kernel, scale),
            out_shape=(field_shape, low_shape) + out_halos,
            in_specs=[VMEM] * 5,
            out_specs=(VMEM,) * (2 + len(out_halos)),
            compiler_params=SMALL,
        )(part, first, third, second, field)

    seen = observed == 1

    def fit(low):
        return jnp.where(seen, against(low, series_factors), 0.0)

    def back(rows_here):
        return jnp.dot(rows_here, series_factors, preferred_element_type=jnp.float32)

    low = time_factors.astype(jnp.bfloat16)
    many, few = fetch(time_factors, time_factors)
    kept = jnp.where(seen, series_values, jnp.zeros((), jnp.bfloat16))
    local = back(kept) - back(fit(low).astype(jnp.bfloat16))
    part = penalty(-penalty_weight, time_factors, many, few, local)
    power0, low, many, few = series_sum(-ridge_weight, part, time_factors, halo_shapes)

    def image(field, low, many, few, out_halos):
        many, few = fetch(many, few)
        local = back(fit(low).astype(jnp.bfloat16))
        part = penalty(penalty_weight, field, many, few, local)
        return series_sum(ridge_weight, part, field, out_halos)

    power1, low, many, few = image(power0, low, many, few, halo_shapes)
    power2, low, many = image(power1, low, many, few, (many_shape,))
    many = lax.ppermute(many, both, last_route)
    fitted = fit(low)
    squares = jnp.sum(fitted * fitted, axis=0, keepdims=True)
    packed = pl.pallas_call(
        functools.partial(products_kernel, 1.0 / n_series),
        out_shape=jax.ShapeDtypeStruct((8, rank), jnp.float32),
        in_specs=[VMEM] * 4,
        out_specs=VMEM,
        compiler_params=SMALL,
    )(squares, power0, power1, power2)
    spread = pl.pallas_call(
        functools.partial(moments_kernel, last_time),
        out_shape=jax.ShapeDtypeStruct((everyone, 1, rank), jnp.float32),
        in_specs=[VMEM] * 4,
        out_specs=VMEM,
        scratch_shapes=lag_scratch,
        compiler_params=SMALL,
    )(packed, power2, many, lag_weights)
    gathered = lax.all_to_all(spread, both, split_axis=0, concat_axis=0, tiled=True)
    final, misfit = pl.pallas_call(
        update_kernel,
        out_shape=(field_shape, jax.ShapeDtypeStruct((n_tm, rows, rank), jnp.bfloat16)),
        in_specs=[VMEM] * 7,
        out_specs=(VMEM, VMEM),
        compiler_params=SMALL,
    )(gathered, time_factors, power0, power1, power2, series_values, series_factors)
    misfit = lax.all_to_all(misfit, "tm", split_axis=0, concat_axis=0, tiled=True)
    return final, misfit.reshape(n_tm * rows, rank)


def solution(mesh):
    placed = (P("tm", "series"), P("tm", "series"), P("series", None), P("tm", None), P())
    return jax.shard_map(
        on_device,
        mesh=mesh,
        in_specs=placed,
        out_specs=(P("tm", None), P(None, ("series", "tm"))),
        check_vma=False,
    )
```

```python
import functools

import jax
import jax.numpy as jnp
from jax import lax
from jax.experimental import pallas as pl
from jax.experimental.pallas import tpu as pltpu
from jax.sharding import PartitionSpec as P

SHORT = 24
SEASON = 168
LAGS = list(range(1, SHORT + 1)) + [SEASON]
MANY = 48
EDGE = SEASON + 8
data_weight = 2.0
penalty_weight = 0.5
ridge_weight = 0.2

VMEM = pl.BlockSpec(memory_space=pltpu.VMEM)
SMALL = pltpu.CompilerParams(vmem_limit_bytes=2 << 20)


def against(left_rows, factors):
    return lax.dot_general(
        left_rows, factors, (((1,), (1,)), ((), ())), preferred_element_type=jnp.float32
    )


def lag_product(blocks, weights_ref, window, short, last_time):
    rank = weights_ref.shape[1]
    rows = window.shape[0] - 2 * EDGE
    first_time = lax.axis_index("tm") * rows
    window[...] = jnp.zeros_like(window)
    for start, block in blocks:
        if not isinstance(start, int):
            start = pl.multiple_of(start, 8)
        window[pl.ds(start, block.shape[0]), :] = block

    def weight(number):
        return weights_ref[number : number + 1, :]

    def lagged(start, count):
        base = EDGE + start
        result = window[base : base + count, :]
        for number, lag in enumerate(LAGS):
            result = result - weight(number) * window[base - lag : base - lag + count, :]
        stamp = first_time + start + lax.broadcasted_iota(jnp.int32, (count, rank), 0)
        return jnp.where(stamp < last_time, result, 0.0)

    short[...] = lagged(0, rows + SHORT)
    result = short[0:rows, :] - weight(SHORT) * lagged(SEASON, rows)
    for number in range(SHORT):
        lag = LAGS[number]
        result = result - weight(number) * short[lag : lag + rows, :]
    return result


def penalty_kernel(
    scale, last_time, field_ref, many_ref, few_ref, weights_ref, local_ref,
    part_ref, window, short,
):
    here = lax.axis_index("series")
    many_at = jnp.where(
        here == 0, 0, jnp.where(here == 1, 368, jnp.where(here == 2, 48, 320))
    )
    blocks = [
        (EDGE, jnp.where(here == 0, field_ref[...], 0.0)),
        (many_at, long_rows(here, many_ref[...].astype(jnp.float32))),
        (jnp.where(here == 3, 240, 128), short_rows(here, few_ref[...].astype(jnp.float32))),
    ]
    product = lag_product(blocks, weights_ref, window, short, last_time)
    part_ref[...] = data_weight * local_ref[...] + scale * product


def rows_for(late, field):
    rows = field.shape[0]
    if rows == MANY:
        return field
    return jnp.where(late, field[rows - MANY :], field[:MANY])


def long_rows(here, field):
    return rows_for(jnp.logical_or(here == 0, here == 3), field)


def short_rows(here, field):
    return rows_for(here == 2, field)


def sum_kernel(
    scale, own_ref, first_ref, third_ref, second_ref, field_ref,
    total_ref, low_ref, *halo_refs,
):
    here = lax.axis_index("series")
    total = (own_ref[...] + second_ref[...]) + (first_ref[...] + third_ref[...])
    total = total + scale * field_ref[...]
    total_ref[...] = total
    low_ref[...] = total.astype(jnp.bfloat16)
    halo_refs[0][...] = long_rows(here, total).astype(jnp.bfloat16)
    if len(halo_refs) > 1:
        halo_refs[1][...] = short_rows(here, total).astype(jnp.bfloat16)


def place_sums(sums, first, rank):
    lane = lax.broadcasted_iota(jnp.int32, (1, rank), 1)
    packed = jnp.zeros((1, rank), jnp.float32)
    for number, value in enumerate(sums):
        packed = jnp.where(lane == first + number, value, packed)
    return packed


def inner(left, right):
    return jnp.sum(jnp.sum(left * right, axis=0, keepdims=True), axis=1, keepdims=True)


def products_kernel(share, squares_ref, zero_ref, one_ref, two_ref, packed_ref):
    zero, one, two = zero_ref[...], one_ref[...], two_ref[...]
    sums = [
        inner(zero, zero),
        inner(zero, one),
        inner(zero, two),
        inner(one, one),
        inner(one, two),
        inner(two, two),
    ]
    squares = jnp.sum(squares_ref[...], axis=1, keepdims=True)
    packed = share * place_sums(sums, 0, zero.shape[1])
    packed = packed + place_sums([data_weight * squares], len(sums), zero.shape[1])
    packed_ref[...] = jnp.broadcast_to(packed, packed_ref.shape)


def moments_kernel(
    last_time, packed_ref, two_ref, many_ref,
    weights_ref, spread_ref, window, short,
):
    two = two_ref[...]
    here = lax.axis_index("series")
    many_at = jnp.where(here == 1, 368, jnp.where(here == 2, 240, 320))
    blocks = [
        (EDGE, jnp.where(here == 0, two, 0.0)),
        (many_at, jnp.where(here == 0, 0.0, 2.0 * many_ref[...].astype(jnp.float32))),
    ]
    product = lag_product(blocks, weights_ref, window, short, last_time)
    quadratic = penalty_weight * inner(two, product)
    packed = packed_ref[0:1, :] + place_sums([quadratic], 6, two.shape[1])
    spread_ref[...] = jnp.broadcast_to(packed[None], spread_ref.shape)


def update_kernel(
    gathered_ref, start_ref, zero_ref, one_ref, two_ref, values_ref, factors_ref,
    final_ref, misfit_ref,
):
    total = gathered_ref[...]
    while total.shape[0] > 1:
        half = total.shape[0] // 2
        total = total[:half] + total[half:]
    total = total[0]
    lane = lax.broadcasted_iota(jnp.int32, total.shape, 1)

    def pick(number):
        return jnp.sum(jnp.where(lane == number, total, 0.0), axis=1, keepdims=True)

    m00, m01, m02, m11, m12, m22, m23 = [pick(number) for number in range(7)]
    m23 = m23 + ridge_weight * m22
    alpha0 = m00 / m01
    norm1 = m00 - 2.0 * alpha0 * m01 + alpha0 * alpha0 * m11
    g0 = 1.0 + norm1 / m00
    curvature1 = g0 * g0 * m01 - g0 * alpha0 * (m02 + m11) + alpha0 * alpha0 * m12
    alpha1 = norm1 / curvature1
    a = -(alpha0 + alpha1 * g0)
    b = alpha0 * alpha1
    norm2 = m00 + a * a * m11 + b * b * m22 + 2.0 * (a * m01 + b * m02 + a * b * m12)
    beta1 = norm2 / norm1
    c = 1.0 + beta1 * g0
    d = a - beta1 * alpha0
    curvature2 = (
        c * c * m01
        + c * d * (m02 + m11)
        + 2.0 * c * b * m12
        + d * d * m12
        + 2.0 * d * b * m22
        + b * b * m23
    )
    alpha2 = norm2 / curvature2
    k0 = alpha0 + alpha1 * g0 + alpha2 * c
    k1 = alpha2 * d - alpha1 * alpha0
    k2 = alpha2 * b
    final = start_ref[...] + (k0 * zero_ref[...] + k1 * one_ref[...] + k2 * two_ref[...])
    final_ref[...] = final
    low = final.astype(jnp.bfloat16)
    lanes = misfit_ref.shape[2]
    for first in range(0, values_ref.shape[1], 2 * lanes):
        columns = slice(first, first + 2 * lanes)
        fitted = against(low, factors_ref[columns, :])
        block = (values_ref[:, columns].astype(jnp.float32) - fitted).astype(jnp.bfloat16)
        misfit_ref[first // lanes] = block[:, :lanes]
        misfit_ref[first // lanes + 1] = block[:, lanes:]


def on_device(series_values, observed, series_factors, time_factors, lag_weights):
    rows, rank = time_factors.shape
    n_tm = lax.axis_size("tm")
    n_series = lax.axis_size("series")
    everyone = n_tm * n_series
    last_time = n_tm * rows
    field_shape = jax.ShapeDtypeStruct((rows, rank), jnp.float32)
    many_shape = jax.ShapeDtypeStruct((MANY, rank), jnp.bfloat16)
    few_shape = jax.ShapeDtypeStruct((MANY, rank), jnp.bfloat16)
    halo_shapes = (many_shape, few_shape)
    low_shape = jax.ShapeDtypeStruct((rows, rank), jnp.bfloat16)
    lag_scratch = [
        pltpu.VMEM((2 * EDGE + rows, rank), jnp.float32),
        pltpu.VMEM((rows + SHORT, rank), jnp.float32),
    ]

    def route(steps):
        pairs = []
        for column, step in enumerate(steps):
            if step is None:
                continue
            for source in range(n_tm):
                target = source + step
                if 0 <= target < n_tm:
                    pairs.append((source * n_series + column, target * n_series + column))
        return pairs

    many_route = route([3, -3, 2, -2])
    few_route = route([None, None, 1, -1])
    last_route = route([None, -3, -1, -2])
    both = ("tm", "series")

    def fetch(many, few):
        few = lax.ppermute(few, both, few_route)
        return lax.ppermute(many, both, many_route), few

    def penalty(scale, field, many, few, local):
        return pl.pallas_call(
            functools.partial(penalty_kernel, scale, last_time),
            out_shape=field_shape,
            in_specs=[VMEM] * 5,
            out_specs=VMEM,
            scratch_shapes=lag_scratch,
            compiler_params=SMALL,
        )(field, many, few, lag_weights, local)

    def series_sum(scale, part, field, out_halos):
        def moved(distance):
            pairs = [(i, (i + distance) % n_series) for i in range(n_series)]
            return lax.ppermute(part, "series", pairs)

        first, third = moved(1), moved(3)
        second = moved(2)
        return pl.pallas_call(
            functools.partial(sum_kernel, scale),
            out_shape=(field_shape, low_shape) + out_halos,
            in_specs=[VMEM] * 5,
            out_specs=(VMEM,) * (2 + len(out_halos)),
            compiler_params=SMALL,
        )(part, first, third, second, field)

    seen = observed == 1

    def fit(low):
        return jnp.where(seen, against(low, series_factors), 0.0)

    def back(rows_here):
        return jnp.dot(rows_here, series_factors, preferred_element_type=jnp.float32)

    low = time_factors.astype(jnp.bfloat16)
    many, few = fetch(time_factors, time_factors)
    kept = jnp.where(seen, series_values, jnp.zeros((), jnp.bfloat16))
    local = back(kept) - back(fit(low).astype(jnp.bfloat16))
    part = penalty(-penalty_weight, time_factors, many, few, local)
    power0, low, many, few = series_sum(-ridge_weight, part, time_factors, halo_shapes)

    def image(field, low, many, few, out_halos):
        many, few = fetch(many, few)
        local = back(fit(low).astype(jnp.bfloat16))
        part = penalty(penalty_weight, field, many, few, local)
        return series_sum(ridge_weight, part, field, out_halos)

    power1, low, many, few = image(power0, low, many, few, halo_shapes)
    power2, low, many = image(power1, low, many, few, (many_shape,))
    many = lax.ppermute(many, both, last_route)
    fitted = fit(low)
    squares = jnp.sum(fitted * fitted, axis=0, keepdims=True)
    packed = pl.pallas_call(
        functools.partial(products_kernel, 1.0 / n_series),
        out_shape=jax.ShapeDtypeStruct((8, rank), jnp.float32),
        in_specs=[VMEM] * 4,
        out_specs=VMEM,
        compiler_params=SMALL,
    )(squares, power0, power1, power2)
    spread = pl.pallas_call(
        functools.partial(moments_kernel, last_time),
        out_shape=jax.ShapeDtypeStruct((everyone, 1, rank), jnp.float32),
        in_specs=[VMEM] * 4,
        out_specs=VMEM,
        scratch_shapes=lag_scratch,
        compiler_params=SMALL,
    )(packed, power2, many, lag_weights)
    gathered = lax.all_to_all(spread, both, split_axis=0, concat_axis=0, tiled=True)
    final, misfit = pl.pallas_call(
        update_kernel,
        out_shape=(field_shape, jax.ShapeDtypeStruct((n_tm, rows, rank), jnp.bfloat16)),
        in_specs=[VMEM] * 7,
        out_specs=(VMEM, VMEM),
        compiler_params=SMALL,
    )(gathered, time_factors, power0, power1, power2, series_values, series_factors)
    misfit = lax.all_to_all(misfit, "tm", split_axis=0, concat_axis=0, tiled=True)
    return final, misfit.reshape(n_tm * rows, rank)


def solution(mesh):
    placed = (P("tm", "series"), P("tm", "series"), P("series", None), P("tm", None), P())
    return jax.shard_map(
        on_device,
        mesh=mesh,
        in_specs=placed,
        out_specs=(P("tm", None), P(None, ("series", "tm"))),
        check_vma=False,
    )
```

```python
import functools

import jax
import jax.numpy as jnp
from jax import lax
from jax.experimental import pallas as pl
from jax.experimental.pallas import tpu as pltpu
from jax.sharding import PartitionSpec as P

SHORT = 24
SEASON = 168
LAGS = list(range(1, SHORT + 1)) + [SEASON]
MANY = 48
EDGE = SEASON + 8
data_weight = 2.0
penalty_weight = 0.5
ridge_weight = 0.2

VMEM = pl.BlockSpec(memory_space=pltpu.VMEM)
SMALL = pltpu.CompilerParams(vmem_limit_bytes=2 << 20)


def against(left_rows, factors):
    return lax.dot_general(
        left_rows, factors, (((1,), (1,)), ((), ())), preferred_element_type=jnp.float32
    )


def lag_product(blocks, weights_ref, window, short, last_time):
    rank = weights_ref.shape[1]
    rows = window.shape[0] - 2 * EDGE
    first_time = lax.axis_index("tm") * rows
    window[...] = jnp.zeros_like(window)
    for start, block in blocks:
        if not isinstance(start, int):
            start = pl.multiple_of(start, 8)
        window[pl.ds(start, block.shape[0]), :] = block

    def weight(number):
        return weights_ref[number : number + 1, :]

    def lagged(start, count):
        base = EDGE + start
        result = window[base : base + count, :]
        for number, lag in enumerate(LAGS):
            result = result - weight(number) * window[base - lag : base - lag + count, :]
        stamp = first_time + start + lax.broadcasted_iota(jnp.int32, (count, rank), 0)
        return jnp.where(stamp < last_time, result, 0.0)

    short[...] = lagged(0, rows + SHORT)
    result = short[0:rows, :] - weight(SHORT) * lagged(SEASON, rows)
    for number in range(SHORT):
        lag = LAGS[number]
        result = result - weight(number) * short[lag : lag + rows, :]
    return result


def penalty_kernel(
    scale, last_time, field_ref, many_ref, few_ref, weights_ref, local_ref,
    part_ref, window, short,
):
    here = lax.axis_index("series")
    many_at = jnp.where(
        here == 0, 0, jnp.where(here == 1, 368, jnp.where(here == 2, 48, 320))
    )
    blocks = [
        (EDGE, jnp.where(here == 0, field_ref[...], 0.0)),
        (many_at, long_rows(here, many_ref[...].astype(jnp.float32))),
        (jnp.where(here == 3, 240, 128), short_rows(here, few_ref[...].astype(jnp.float32))),
    ]
    product = lag_product(blocks, weights_ref, window, short, last_time)
    part_ref[...] = data_weight * local_ref[...] + scale * product


def rows_for(late, field):
    rows = field.shape[0]
    if rows == MANY:
        return field
    return jnp.where(late, field[rows - MANY :], field[:MANY])


def long_rows(here, field):
    return rows_for(jnp.logical_or(here == 0, here == 3), field)


def short_rows(here, field):
    return rows_for(here == 2, field)


def sum_kernel(
    scale, own_ref, first_ref, third_ref, second_ref, field_ref,
    total_ref, low_ref, *halo_refs,
):
    here = lax.axis_index("series")
    total = (own_ref[...] + second_ref[...]) + (first_ref[...] + third_ref[...])
    total = total + scale * field_ref[...]
    total_ref[...] = total
    low_ref[...] = total.astype(jnp.bfloat16)
    halo_refs[0][...] = long_rows(here, total).astype(jnp.bfloat16)
    if len(halo_refs) > 1:
        halo_refs[1][...] = short_rows(here, total).astype(jnp.bfloat16)


def place_sums(sums, first, rank):
    lane = lax.broadcasted_iota(jnp.int32, (1, rank), 1)
    packed = jnp.zeros((1, rank), jnp.float32)
    for number, value in enumerate(sums):
        packed = jnp.where(lane == first + number, value, packed)
    return packed


def inner(left, right):
    return jnp.sum(jnp.sum(left * right, axis=0, keepdims=True), axis=1, keepdims=True)


def products_kernel(share, squares_ref, zero_ref, one_ref, two_ref, packed_ref):
    zero, one, two = zero_ref[...], one_ref[...], two_ref[...]
    sums = [
        inner(zero, zero),
        inner(zero, one),
        inner(zero, two),
        inner(one, one),
        inner(one, two),
        inner(two, two),
    ]
    squares = jnp.sum(squares_ref[...], axis=1, keepdims=True)
    packed = share * place_sums(sums, 0, zero.shape[1])
    packed = packed + place_sums([data_weight * squares], len(sums), zero.shape[1])
    packed_ref[...] = jnp.broadcast_to(packed, packed_ref.shape)


def moments_kernel(
    last_time, packed_ref, two_ref, many_ref,
    weights_ref, spread_ref, window, short,
):
    two = two_ref[...]
    here = lax.axis_index("series")
    many_at = jnp.where(here == 1, 368, jnp.where(here == 2, 240, 320))
    blocks = [
        (EDGE, jnp.where(here == 0, two, 0.0)),
        (many_at, jnp.where(here == 0, 0.0, 2.0 * many_ref[...].astype(jnp.float32))),
    ]
    product = lag_product(blocks, weights_ref, window, short, last_time)
    quadratic = penalty_weight * inner(two, product)
    packed = packed_ref[0:1, :] + place_sums([quadratic], 6, two.shape[1])
    spread_ref[...] = jnp.broadcast_to(packed[None], spread_ref.shape)


def update_kernel(
    gathered_ref, start_ref, zero_ref, one_ref, two_ref, values_ref, factors_ref,
    steps_ref, misfit_ref,
):
    total = gathered_ref[...]
    while total.shape[0] > 1:
        half = total.shape[0] // 2
        total = total[:half] + total[half:]
    total = total[0]
    lane = lax.broadcasted_iota(jnp.int32, total.shape, 1)

    def pick(number):
        return jnp.sum(jnp.where(lane == number, total, 0.0), axis=1, keepdims=True)

    m00, m01, m02, m11, m12, m22, m23 = [pick(number) for number in range(7)]
    m23 = m23 + ridge_weight * m22
    alpha0 = m00 / m01
    norm1 = m00 - 2.0 * alpha0 * m01 + alpha0 * alpha0 * m11
    g0 = 1.0 + norm1 / m00
    curvature1 = g0 * g0 * m01 - g0 * alpha0 * (m02 + m11) + alpha0 * alpha0 * m12
    alpha1 = norm1 / curvature1
    a = -(alpha0 + alpha1 * g0)
    b = alpha0 * alpha1
    norm2 = m00 + a * a * m11 + b * b * m22 + 2.0 * (a * m01 + b * m02 + a * b * m12)
    beta1 = norm2 / norm1
    c = 1.0 + beta1 * g0
    d = a - beta1 * alpha0
    curvature2 = (
        c * c * m01
        + c * d * (m02 + m11)
        + 2.0 * c * b * m12
        + d * d * m12
        + 2.0 * d * b * m22
        + b * b * m23
    )
    alpha2 = norm2 / curvature2
    k0 = alpha0 + alpha1 * g0 + alpha2 * c
    k1 = alpha2 * d - alpha1 * alpha0
    k2 = alpha2 * b
    final = start_ref[...] + (k0 * zero_ref[...] + k1 * one_ref[...] + k2 * two_ref[...])
    number = lax.broadcasted_iota(jnp.int32, steps_ref.shape, 0)
    steps_ref[...] = jnp.where(number == 0, k0, jnp.where(number == 1, k1, k2))
    low = final.astype(jnp.bfloat16)
    lanes = misfit_ref.shape[2]
    for first in range(0, values_ref.shape[1], 2 * lanes):
        columns = slice(first, first + 2 * lanes)
        fitted = against(low, factors_ref[columns, :])
        block = (values_ref[:, columns].astype(jnp.float32) - fitted).astype(jnp.bfloat16)
        misfit_ref[first // lanes] = block[:, :lanes]
        misfit_ref[first // lanes + 1] = block[:, lanes:]


def final_kernel(steps_ref, start_ref, zero_ref, one_ref, two_ref, final_ref):
    k0, k1, k2 = [steps_ref[number : number + 1, :] for number in range(3)]
    final_ref[...] = start_ref[...] + (
        k0 * zero_ref[...] + k1 * one_ref[...] + k2 * two_ref[...]
    )


def on_device(series_values, observed, series_factors, time_factors, lag_weights):
    rows, rank = time_factors.shape
    n_tm = lax.axis_size("tm")
    n_series = lax.axis_size("series")
    everyone = n_tm * n_series
    last_time = n_tm * rows
    field_shape = jax.ShapeDtypeStruct((rows, rank), jnp.float32)
    many_shape = jax.ShapeDtypeStruct((MANY, rank), jnp.bfloat16)
    few_shape = jax.ShapeDtypeStruct((MANY, rank), jnp.bfloat16)
    halo_shapes = (many_shape, few_shape)
    low_shape = jax.ShapeDtypeStruct((rows, rank), jnp.bfloat16)
    lag_scratch = [
        pltpu.VMEM((2 * EDGE + rows, rank), jnp.float32),
        pltpu.VMEM((rows + SHORT, rank), jnp.float32),
    ]

    def route(steps):
        pairs = []
        for column, step in enumerate(steps):
            if step is None:
                continue
            for source in range(n_tm):
                target = source + step
                if 0 <= target < n_tm:
                    pairs.append((source * n_series + column, target * n_series + column))
        return pairs

    many_route = route([3, -3, 2, -2])
    few_route = route([None, None, 1, -1])
    last_route = route([None, -3, -1, -2])
    both = ("tm", "series")

    def fetch(many, few):
        few = lax.ppermute(few, both, few_route)
        return lax.ppermute(many, both, many_route), few

    def penalty(scale, field, many, few, local):
        return pl.pallas_call(
            functools.partial(penalty_kernel, scale, last_time),
            out_shape=field_shape,
            in_specs=[VMEM] * 5,
            out_specs=VMEM,
            scratch_shapes=lag_scratch,
            compiler_params=SMALL,
        )(field, many, few, lag_weights, local)

    def series_sum(scale, part, field, out_halos):
        def moved(distance):
            pairs = [(i, (i + distance) % n_series) for i in range(n_series)]
            return lax.ppermute(part, "series", pairs)

        first, third = moved(1), moved(3)
        second = moved(2)
        return pl.pallas_call(
            functools.partial(sum_kernel, scale),
            out_shape=(field_shape, low_shape) + out_halos,
            in_specs=[VMEM] * 5,
            out_specs=(VMEM,) * (2 + len(out_halos)),
            compiler_params=SMALL,
        )(part, first, third, second, field)

    seen = observed == 1

    def fit(low):
        return jnp.where(seen, against(low, series_factors), 0.0)

    def back(rows_here):
        return jnp.dot(rows_here, series_factors, preferred_element_type=jnp.float32)

    low = time_factors.astype(jnp.bfloat16)
    many, few = fetch(time_factors, time_factors)
    kept = jnp.where(seen, series_values, jnp.zeros((), jnp.bfloat16))
    local = back(kept) - back(fit(low).astype(jnp.bfloat16))
    part = penalty(-penalty_weight, time_factors, many, few, local)
    power0, low, many, few = series_sum(-ridge_weight, part, time_factors, halo_shapes)

    def image(field, low, many, few, out_halos):
        many, few = fetch(many, few)
        local = back(fit(low).astype(jnp.bfloat16))
        part = penalty(penalty_weight, field, many, few, local)
        return series_sum(ridge_weight, part, field, out_halos)

    power1, low, many, few = image(power0, low, many, few, halo_shapes)
    power2, low, many = image(power1, low, many, few, (many_shape,))
    many = lax.ppermute(many, both, last_route)
    fitted = fit(low)
    squares = jnp.sum(fitted * fitted, axis=0, keepdims=True)
    packed = pl.pallas_call(
        functools.partial(products_kernel, 1.0 / n_series),
        out_shape=jax.ShapeDtypeStruct((8, rank), jnp.float32),
        in_specs=[VMEM] * 4,
        out_specs=VMEM,
        compiler_params=SMALL,
    )(squares, power0, power1, power2)
    spread = pl.pallas_call(
        functools.partial(moments_kernel, last_time),
        out_shape=jax.ShapeDtypeStruct((everyone, 1, rank), jnp.float32),
        in_specs=[VMEM] * 4,
        out_specs=VMEM,
        scratch_shapes=lag_scratch,
        compiler_params=SMALL,
    )(packed, power2, many, lag_weights)
    gathered = lax.all_to_all(spread, both, split_axis=0, concat_axis=0, tiled=True)
    steps, misfit = pl.pallas_call(
        update_kernel,
        out_shape=(jax.ShapeDtypeStruct((8, rank), jnp.float32), jax.ShapeDtypeStruct((n_tm, rows, rank), jnp.bfloat16)),
        in_specs=[VMEM] * 7,
        out_specs=(VMEM, VMEM),
        compiler_params=SMALL,
    )(gathered, time_factors, power0, power1, power2, series_values, series_factors)
    final = pl.pallas_call(
        final_kernel,
        out_shape=field_shape,
        in_specs=[VMEM] * 5,
        out_specs=VMEM,
        compiler_params=SMALL,
    )(steps, time_factors, power0, power1, power2)
    misfit = lax.all_to_all(misfit, "tm", split_axis=0, concat_axis=0, tiled=True)
    return final, misfit.reshape(n_tm * rows, rank)


def solution(mesh):
    placed = (P("tm", "series"), P("tm", "series"), P("series", None), P("tm", None), P())
    return jax.shard_map(
        on_device,
        mesh=mesh,
        in_specs=placed,
        out_specs=(P("tm", None), P(None, ("series", "tm"))),
        check_vma=False,
    )
```

```python
import functools

import jax
import jax.numpy as jnp
from jax import lax
from jax.experimental import pallas as pl
from jax.experimental.pallas import tpu as pltpu
from jax.sharding import PartitionSpec as P

SHORT = 24
SEASON = 168
LAGS = list(range(1, SHORT + 1)) + [SEASON]
MANY = 48
EDGE = SEASON + 8
data_weight = 2.0
penalty_weight = 0.5
ridge_weight = 0.2

VMEM = pl.BlockSpec(memory_space=pltpu.VMEM)
SMALL = pltpu.CompilerParams(vmem_limit_bytes=2 << 20)


def against(left_rows, factors):
    return lax.dot_general(
        left_rows, factors, (((1,), (1,)), ((), ())), preferred_element_type=jnp.float32
    )


def lag_product(blocks, weights_ref, window, short, last_time):
    rank = weights_ref.shape[1]
    rows = window.shape[0] - 2 * EDGE
    first_time = lax.axis_index("tm") * rows
    window[...] = jnp.zeros_like(window)
    for start, block in blocks:
        if not isinstance(start, int):
            start = pl.multiple_of(start, 8)
        window[pl.ds(start, block.shape[0]), :] = block

    def weight(number):
        return weights_ref[number : number + 1, :]

    def lagged(start, count):
        base = EDGE + start
        result = window[base : base + count, :]
        for number, lag in enumerate(LAGS):
            result = result - weight(number) * window[base - lag : base - lag + count, :]
        stamp = first_time + start + lax.broadcasted_iota(jnp.int32, (count, rank), 0)
        return jnp.where(stamp < last_time, result, 0.0)

    short[...] = lagged(0, rows + SHORT)
    result = short[0:rows, :] - weight(SHORT) * lagged(SEASON, rows)
    for number in range(SHORT):
        lag = LAGS[number]
        result = result - weight(number) * short[lag : lag + rows, :]
    return result


def penalty_kernel(
    scale, last_time, field_ref, few_ref, many_ref, weights_ref, local_ref,
    part_ref, window, short,
):
    here = lax.axis_index("series")
    many_at = jnp.where(
        here == 0, 0, jnp.where(here == 1, 368, jnp.where(here == 2, 48, 320))
    )
    blocks = [
        (EDGE, jnp.where(here == 0, field_ref[...], 0.0)),
        (many_at, long_rows(here, many_ref[...].astype(jnp.float32))),
        (jnp.where(here == 3, 240, 128), short_rows(here, few_ref[...].astype(jnp.float32))),
    ]
    product = lag_product(blocks, weights_ref, window, short, last_time)
    part_ref[...] = data_weight * local_ref[...] + scale * product


def rows_for(late, field):
    rows = field.shape[0]
    if rows == MANY:
        return field
    return jnp.where(late, field[rows - MANY :], field[:MANY])


def long_rows(here, field):
    return rows_for(jnp.logical_or(here == 0, here == 3), field)


def short_rows(here, field):
    return rows_for(here == 2, field)


def sum_kernel(
    scale, own_ref, first_ref, third_ref, second_ref, field_ref,
    total_ref, low_ref, *halo_refs,
):
    here = lax.axis_index("series")
    total = (own_ref[...] + second_ref[...]) + (first_ref[...] + third_ref[...])
    total = total + scale * field_ref[...]
    total_ref[...] = total
    low_ref[...] = total.astype(jnp.bfloat16)
    halo_refs[0][...] = long_rows(here, total).astype(jnp.bfloat16)
    if len(halo_refs) > 1:
        halo_refs[1][...] = short_rows(here, total).astype(jnp.bfloat16)


def place_sums(sums, first, rank):
    lane = lax.broadcasted_iota(jnp.int32, (1, rank), 1)
    packed = jnp.zeros((1, rank), jnp.float32)
    for number, value in enumerate(sums):
        packed = jnp.where(lane == first + number, value, packed)
    return packed


def inner(left, right):
    return jnp.sum(jnp.sum(left * right, axis=0, keepdims=True), axis=1, keepdims=True)


def products_kernel(share, squares_ref, zero_ref, one_ref, two_ref, packed_ref):
    zero, one, two = zero_ref[...], one_ref[...], two_ref[...]
    sums = [
        inner(zero, zero),
        inner(zero, one),
        inner(zero, two),
        inner(one, one),
        inner(one, two),
        inner(two, two),
    ]
    squares = jnp.sum(squares_ref[...], axis=1, keepdims=True)
    packed = share * place_sums(sums, 0, zero.shape[1])
    packed = packed + place_sums([data_weight * squares], len(sums), zero.shape[1])
    packed_ref[...] = jnp.broadcast_to(packed, packed_ref.shape)


def moments_kernel(
    last_time, packed_ref, two_ref, many_ref,
    weights_ref, spread_ref, window, short,
):
    two = two_ref[...]
    here = lax.axis_index("series")
    many_at = jnp.where(here == 1, 368, jnp.where(here == 2, 240, 320))
    blocks = [
        (EDGE, jnp.where(here == 0, two, 0.0)),
        (many_at, jnp.where(here == 0, 0.0, 2.0 * many_ref[...].astype(jnp.float32))),
    ]
    product = lag_product(blocks, weights_ref, window, short, last_time)
    quadratic = penalty_weight * inner(two, product)
    packed = packed_ref[0:1, :] + place_sums([quadratic], 6, two.shape[1])
    spread_ref[...] = jnp.broadcast_to(packed[None], spread_ref.shape)


def update_kernel(
    gathered_ref, start_ref, zero_ref, one_ref, two_ref, values_ref, factors_ref,
    final_ref, misfit_ref,
):
    total = gathered_ref[...]
    while total.shape[0] > 1:
        half = total.shape[0] // 2
        total = total[:half] + total[half:]
    total = total[0]
    lane = lax.broadcasted_iota(jnp.int32, total.shape, 1)

    def pick(number):
        return jnp.sum(jnp.where(lane == number, total, 0.0), axis=1, keepdims=True)

    m00, m01, m02, m11, m12, m22, m23 = [pick(number) for number in range(7)]
    m23 = m23 + ridge_weight * m22
    alpha0 = m00 / m01
    norm1 = m00 - 2.0 * alpha0 * m01 + alpha0 * alpha0 * m11
    g0 = 1.0 + norm1 / m00
    curvature1 = g0 * g0 * m01 - g0 * alpha0 * (m02 + m11) + alpha0 * alpha0 * m12
    alpha1 = norm1 / curvature1
    a = -(alpha0 + alpha1 * g0)
    b = alpha0 * alpha1
    norm2 = m00 + a * a * m11 + b * b * m22 + 2.0 * (a * m01 + b * m02 + a * b * m12)
    beta1 = norm2 / norm1
    c = 1.0 + beta1 * g0
    d = a - beta1 * alpha0
    curvature2 = (
        c * c * m01
        + c * d * (m02 + m11)
        + 2.0 * c * b * m12
        + d * d * m12
        + 2.0 * d * b * m22
        + b * b * m23
    )
    alpha2 = norm2 / curvature2
    k0 = alpha0 + alpha1 * g0 + alpha2 * c
    k1 = alpha2 * d - alpha1 * alpha0
    k2 = alpha2 * b
    final = start_ref[...] + (k0 * zero_ref[...] + k1 * one_ref[...] + k2 * two_ref[...])
    final_ref[...] = final
    low = final.astype(jnp.bfloat16)
    lanes = misfit_ref.shape[2]
    for first in range(0, values_ref.shape[1], 2 * lanes):
        columns = slice(first, first + 2 * lanes)
        fitted = against(low, factors_ref[columns, :])
        block = (values_ref[:, columns].astype(jnp.float32) - fitted).astype(jnp.bfloat16)
        misfit_ref[first // lanes] = block[:, :lanes]
        misfit_ref[first // lanes + 1] = block[:, lanes:]


def on_device(series_values, observed, series_factors, time_factors, lag_weights):
    rows, rank = time_factors.shape
    n_tm = lax.axis_size("tm")
    n_series = lax.axis_size("series")
    everyone = n_tm * n_series
    last_time = n_tm * rows
    field_shape = jax.ShapeDtypeStruct((rows, rank), jnp.float32)
    many_shape = jax.ShapeDtypeStruct((MANY, rank), jnp.bfloat16)
    few_shape = jax.ShapeDtypeStruct((MANY, rank), jnp.bfloat16)
    halo_shapes = (many_shape, few_shape)
    low_shape = jax.ShapeDtypeStruct((rows, rank), jnp.bfloat16)
    lag_scratch = [
        pltpu.VMEM((2 * EDGE + rows, rank), jnp.float32),
        pltpu.VMEM((rows + SHORT, rank), jnp.float32),
    ]

    def route(steps):
        pairs = []
        for column, step in enumerate(steps):
            if step is None:
                continue
            for source in range(n_tm):
                target = source + step
                if 0 <= target < n_tm:
                    pairs.append((source * n_series + column, target * n_series + column))
        return pairs

    many_route = route([3, -3, 2, -2])
    few_route = route([None, None, 1, -1])
    last_route = route([None, -3, -1, -2])
    both = ("tm", "series")

    def fetch(many, few):
        few = lax.ppermute(few, both, few_route)
        return lax.ppermute(many, both, many_route), few

    def penalty(scale, field, many, few, local):
        return pl.pallas_call(
            functools.partial(penalty_kernel, scale, last_time),
            out_shape=field_shape,
            in_specs=[VMEM] * 5,
            out_specs=VMEM,
            scratch_shapes=lag_scratch,
            compiler_params=SMALL,
        )(field, few, many, lag_weights, local)

    def series_sum(scale, part, field, out_halos):
        def moved(distance):
            pairs = [(i, (i + distance) % n_series) for i in range(n_series)]
            return lax.ppermute(part, "series", pairs)

        first, third = moved(1), moved(3)
        second = moved(2)
        return pl.pallas_call(
            functools.partial(sum_kernel, scale),
            out_shape=(field_shape, low_shape) + out_halos,
            in_specs=[VMEM] * 5,
            out_specs=(VMEM,) * (2 + len(out_halos)),
            compiler_params=SMALL,
        )(part, first, third, second, field)

    seen = observed == 1

    def fit(low):
        return jnp.where(seen, against(low, series_factors), 0.0)

    def back(rows_here):
        return jnp.dot(rows_here, series_factors, preferred_element_type=jnp.float32)

    low = time_factors.astype(jnp.bfloat16)
    many, few = fetch(time_factors, time_factors)
    kept = jnp.where(seen, series_values, jnp.zeros((), jnp.bfloat16))
    local = back(kept) - back(fit(low).astype(jnp.bfloat16))
    part = penalty(-penalty_weight, time_factors, many, few, local)
    power0, low, many, few = series_sum(-ridge_weight, part, time_factors, halo_shapes)

    def image(field, low, many, few, out_halos):
        many, few = fetch(many, few)
        local = back(fit(low).astype(jnp.bfloat16))
        part = penalty(penalty_weight, field, many, few, local)
        return series_sum(ridge_weight, part, field, out_halos)

    power1, low, many, few = image(power0, low, many, few, halo_shapes)
    power2, low, many = image(power1, low, many, few, (many_shape,))
    many = lax.ppermute(many, both, last_route)
    fitted = fit(low)
    squares = jnp.sum(fitted * fitted, axis=0, keepdims=True)
    packed = pl.pallas_call(
        functools.partial(products_kernel, 1.0 / n_series),
        out_shape=jax.ShapeDtypeStruct((8, rank), jnp.float32),
        in_specs=[VMEM] * 4,
        out_specs=VMEM,
        compiler_params=SMALL,
    )(squares, power0, power1, power2)
    spread = pl.pallas_call(
        functools.partial(moments_kernel, last_time),
        out_shape=jax.ShapeDtypeStruct((everyone, 1, rank), jnp.float32),
        in_specs=[VMEM] * 4,
        out_specs=VMEM,
        scratch_shapes=lag_scratch,
        compiler_params=SMALL,
    )(packed, power2, many, lag_weights)
    gathered = lax.all_to_all(spread, both, split_axis=0, concat_axis=0, tiled=True)
    final, misfit = pl.pallas_call(
        update_kernel,
        out_shape=(field_shape, jax.ShapeDtypeStruct((n_tm, rows, rank), jnp.bfloat16)),
        in_specs=[VMEM] * 7,
        out_specs=(VMEM, VMEM),
        compiler_params=SMALL,
    )(gathered, time_factors, power0, power1, power2, series_values, series_factors)
    misfit = lax.all_to_all(misfit, "tm", split_axis=0, concat_axis=0, tiled=True)
    return final, misfit.reshape(n_tm * rows, rank)


def solution(mesh):
    placed = (P("tm", "series"), P("tm", "series"), P("series", None), P("tm", None), P())
    return jax.shard_map(
        on_device,
        mesh=mesh,
        in_specs=placed,
        out_specs=(P("tm", None), P(None, ("series", "tm"))),
        check_vma=False,
    )
```

```python
import functools

import jax
import jax.numpy as jnp
from jax import lax
from jax.experimental import pallas as pl
from jax.experimental.pallas import tpu as pltpu
from jax.sharding import PartitionSpec as P

SHORT = 24
SEASON = 168
LAGS = list(range(1, SHORT + 1)) + [SEASON]
MANY = 48
EDGE = SEASON + 8
data_weight = 2.0
penalty_weight = 0.5
ridge_weight = 0.2

VMEM = pl.BlockSpec(memory_space=pltpu.VMEM)
SMALL = pltpu.CompilerParams(vmem_limit_bytes=2 << 20)


def against(left_rows, factors):
    return lax.dot_general(
        left_rows, factors, (((1,), (1,)), ((), ())), preferred_element_type=jnp.float32
    )


def lag_product(blocks, weights_ref, window, short, last_time):
    rank = weights_ref.shape[1]
    rows = window.shape[0] - 2 * EDGE
    first_time = lax.axis_index("tm") * rows
    window[...] = jnp.zeros_like(window)
    for start, block in blocks:
        if not isinstance(start, int):
            start = pl.multiple_of(start, 8)
        window[pl.ds(start, block.shape[0]), :] = block

    def weight(number):
        return weights_ref[number : number + 1, :]

    def lagged(start, count):
        base = EDGE + start
        result = window[base : base + count, :]
        for number, lag in enumerate(LAGS):
            result = result - weight(number) * window[base - lag : base - lag + count, :]
        stamp = first_time + start + lax.broadcasted_iota(jnp.int32, (count, rank), 0)
        return jnp.where(stamp < last_time, result, 0.0)

    short[...] = lagged(0, rows + SHORT)
    result = short[0:rows, :] - weight(SHORT) * lagged(SEASON, rows)
    for number in range(SHORT):
        lag = LAGS[number]
        result = result - weight(number) * short[lag : lag + rows, :]
    return result


def penalty_kernel(
    scale, last_time, field_ref, many_ref, few_ref, weights_ref, local_ref,
    part_ref, window, short,
):
    here = lax.axis_index("series")
    many_at = jnp.where(
        here == 0, 0, jnp.where(here == 1, 368, jnp.where(here == 2, 48, 320))
    )
    blocks = [
        (EDGE, jnp.where(here == 0, field_ref[...], 0.0)),
        (many_at, long_rows(here, many_ref[...].astype(jnp.float32))),
        (jnp.where(here == 3, 240, 128), short_rows(here, few_ref[...].astype(jnp.float32))),
    ]
    product = lag_product(blocks, weights_ref, window, short, last_time)
    part_ref[...] = data_weight * local_ref[...] + scale * product


def start_penalty_kernel(scale, last_time, field_ref, few_ref, many_ref, *refs):
    penalty_kernel(scale, last_time, field_ref, many_ref, few_ref, *refs)


def rows_for(late, field):
    rows = field.shape[0]
    if rows == MANY:
        return field
    return jnp.where(late, field[rows - MANY :], field[:MANY])


def long_rows(here, field):
    return rows_for(jnp.logical_or(here == 0, here == 3), field)


def short_rows(here, field):
    return rows_for(here == 2, field)


def sum_kernel(
    scale, own_ref, first_ref, third_ref, second_ref, field_ref,
    total_ref, low_ref, *halo_refs,
):
    here = lax.axis_index("series")
    total = (own_ref[...] + second_ref[...]) + (first_ref[...] + third_ref[...])
    total = total + scale * field_ref[...]
    total_ref[...] = total
    low_ref[...] = total.astype(jnp.bfloat16)
    halo_refs[0][...] = long_rows(here, total).astype(jnp.bfloat16)
    if len(halo_refs) > 1:
        halo_refs[1][...] = short_rows(here, total).astype(jnp.bfloat16)


def place_sums(sums, first, rank):
    lane = lax.broadcasted_iota(jnp.int32, (1, rank), 1)
    packed = jnp.zeros((1, rank), jnp.float32)
    for number, value in enumerate(sums):
        packed = jnp.where(lane == first + number, value, packed)
    return packed


def inner(left, right):
    return jnp.sum(jnp.sum(left * right, axis=0, keepdims=True), axis=1, keepdims=True)


def products_kernel(share, squares_ref, zero_ref, one_ref, two_ref, packed_ref):
    zero, one, two = zero_ref[...], one_ref[...], two_ref[...]
    sums = [
        inner(zero, zero),
        inner(zero, one),
        inner(zero, two),
        inner(one, one),
        inner(one, two),
        inner(two, two),
    ]
    squares = jnp.sum(squares_ref[...], axis=1, keepdims=True)
    packed = share * place_sums(sums, 0, zero.shape[1])
    packed = packed + place_sums([data_weight * squares], len(sums), zero.shape[1])
    packed_ref[...] = jnp.broadcast_to(packed, packed_ref.shape)


def moments_kernel(
    last_time, packed_ref, two_ref, many_ref,
    weights_ref, spread_ref, window, short,
):
    two = two_ref[...]
    here = lax.axis_index("series")
    many_at = jnp.where(here == 1, 368, jnp.where(here == 2, 240, 320))
    blocks = [
        (EDGE, jnp.where(here == 0, two, 0.0)),
        (many_at, jnp.where(here == 0, 0.0, 2.0 * many_ref[...].astype(jnp.float32))),
    ]
    product = lag_product(blocks, weights_ref, window, short, last_time)
    quadratic = penalty_weight * inner(two, product)
    packed = packed_ref[0:1, :] + place_sums([quadratic], 6, two.shape[1])
    spread_ref[...] = jnp.broadcast_to(packed[None], spread_ref.shape)


def update_kernel(
    gathered_ref, start_ref, zero_ref, one_ref, two_ref, values_ref, factors_ref,
    final_ref, misfit_ref,
):
    total = gathered_ref[...]
    while total.shape[0] > 1:
        half = total.shape[0] // 2
        total = total[:half] + total[half:]
    total = total[0]
    lane = lax.broadcasted_iota(jnp.int32, total.shape, 1)

    def pick(number):
        return jnp.sum(jnp.where(lane == number, total, 0.0), axis=1, keepdims=True)

    m00, m01, m02, m11, m12, m22, m23 = [pick(number) for number in range(7)]
    m23 = m23 + ridge_weight * m22
    alpha0 = m00 / m01
    norm1 = m00 - 2.0 * alpha0 * m01 + alpha0 * alpha0 * m11
    g0 = 1.0 + norm1 / m00
    curvature1 = g0 * g0 * m01 - g0 * alpha0 * (m02 + m11) + alpha0 * alpha0 * m12
    alpha1 = norm1 / curvature1
    a = -(alpha0 + alpha1 * g0)
    b = alpha0 * alpha1
    norm2 = m00 + a * a * m11 + b * b * m22 + 2.0 * (a * m01 + b * m02 + a * b * m12)
    beta1 = norm2 / norm1
    c = 1.0 + beta1 * g0
    d = a - beta1 * alpha0
    curvature2 = (
        c * c * m01
        + c * d * (m02 + m11)
        + 2.0 * c * b * m12
        + d * d * m12
        + 2.0 * d * b * m22
        + b * b * m23
    )
    alpha2 = norm2 / curvature2
    k0 = alpha0 + alpha1 * g0 + alpha2 * c
    k1 = alpha2 * d - alpha1 * alpha0
    k2 = alpha2 * b
    final = start_ref[...] + (k0 * zero_ref[...] + k1 * one_ref[...] + k2 * two_ref[...])
    final_ref[...] = final
    low = final.astype(jnp.bfloat16)
    lanes = misfit_ref.shape[2]
    for first in range(0, values_ref.shape[1], 2 * lanes):
        columns = slice(first, first + 2 * lanes)
        fitted = against(low, factors_ref[columns, :])
        block = (values_ref[:, columns].astype(jnp.float32) - fitted).astype(jnp.bfloat16)
        misfit_ref[first // lanes] = block[:, :lanes]
        misfit_ref[first // lanes + 1] = block[:, lanes:]


def on_device(series_values, observed, series_factors, time_factors, lag_weights):
    rows, rank = time_factors.shape
    n_tm = lax.axis_size("tm")
    n_series = lax.axis_size("series")
    everyone = n_tm * n_series
    last_time = n_tm * rows
    field_shape = jax.ShapeDtypeStruct((rows, rank), jnp.float32)
    many_shape = jax.ShapeDtypeStruct((MANY, rank), jnp.bfloat16)
    few_shape = jax.ShapeDtypeStruct((MANY, rank), jnp.bfloat16)
    halo_shapes = (many_shape, few_shape)
    low_shape = jax.ShapeDtypeStruct((rows, rank), jnp.bfloat16)
    lag_scratch = [
        pltpu.VMEM((2 * EDGE + rows, rank), jnp.float32),
        pltpu.VMEM((rows + SHORT, rank), jnp.float32),
    ]

    def route(steps):
        pairs = []
        for column, step in enumerate(steps):
            if step is None:
                continue
            for source in range(n_tm):
                target = source + step
                if 0 <= target < n_tm:
                    pairs.append((source * n_series + column, target * n_series + column))
        return pairs

    many_route = route([3, -3, 2, -2])
    few_route = route([None, None, 1, -1])
    last_route = route([None, -3, -1, -2])
    both = ("tm", "series")

    def fetch(many, few):
        few = lax.ppermute(few, both, few_route)
        return lax.ppermute(many, both, many_route), few

    def penalty(scale, field, first, second, local, kernel=penalty_kernel):
        return pl.pallas_call(
            functools.partial(kernel, scale, last_time),
            out_shape=field_shape,
            in_specs=[VMEM] * 5,
            out_specs=VMEM,
            scratch_shapes=lag_scratch,
            compiler_params=SMALL,
        )(field, first, second, lag_weights, local)

    def series_sum(scale, part, field, out_halos):
        def moved(distance):
            pairs = [(i, (i + distance) % n_series) for i in range(n_series)]
            return lax.ppermute(part, "series", pairs)

        first, third = moved(1), moved(3)
        second = moved(2)
        return pl.pallas_call(
            functools.partial(sum_kernel, scale),
            out_shape=(field_shape, low_shape) + out_halos,
            in_specs=[VMEM] * 5,
            out_specs=(VMEM,) * (2 + len(out_halos)),
            compiler_params=SMALL,
        )(part, first, third, second, field)

    seen = observed == 1

    def fit(low):
        return jnp.where(seen, against(low, series_factors), 0.0)

    def back(rows_here):
        return jnp.dot(rows_here, series_factors, preferred_element_type=jnp.float32)

    low = time_factors.astype(jnp.bfloat16)
    many, few = fetch(time_factors, time_factors)
    kept = jnp.where(seen, series_values, jnp.zeros((), jnp.bfloat16))
    local = back(kept) - back(fit(low).astype(jnp.bfloat16))
    part = penalty(-penalty_weight, time_factors, few, many, local, start_penalty_kernel)
    power0, low, many, few = series_sum(-ridge_weight, part, time_factors, halo_shapes)

    def image(field, low, many, few, out_halos):
        many, few = fetch(many, few)
        local = back(fit(low).astype(jnp.bfloat16))
        part = penalty(penalty_weight, field, many, few, local)
        return series_sum(ridge_weight, part, field, out_halos)

    power1, low, many, few = image(power0, low, many, few, halo_shapes)
    power2, low, many = image(power1, low, many, few, (many_shape,))
    many = lax.ppermute(many, both, last_route)
    fitted = fit(low)
    squares = jnp.sum(fitted * fitted, axis=0, keepdims=True)
    packed = pl.pallas_call(
        functools.partial(products_kernel, 1.0 / n_series),
        out_shape=jax.ShapeDtypeStruct((8, rank), jnp.float32),
        in_specs=[VMEM] * 4,
        out_specs=VMEM,
        compiler_params=SMALL,
    )(squares, power0, power1, power2)
    spread = pl.pallas_call(
        functools.partial(moments_kernel, last_time),
        out_shape=jax.ShapeDtypeStruct((everyone, 1, rank), jnp.float32),
        in_specs=[VMEM] * 4,
        out_specs=VMEM,
        scratch_shapes=lag_scratch,
        compiler_params=SMALL,
    )(packed, power2, many, lag_weights)
    gathered = lax.all_to_all(spread, both, split_axis=0, concat_axis=0, tiled=True)
    final, misfit = pl.pallas_call(
        update_kernel,
        out_shape=(field_shape, jax.ShapeDtypeStruct((n_tm, rows, rank), jnp.bfloat16)),
        in_specs=[VMEM] * 7,
        out_specs=(VMEM, VMEM),
        compiler_params=SMALL,
    )(gathered, time_factors, power0, power1, power2, series_values, series_factors)
    misfit = lax.all_to_all(misfit, "tm", split_axis=0, concat_axis=0, tiled=True)
    return final, misfit.reshape(n_tm * rows, rank)


def solution(mesh):
    placed = (P("tm", "series"), P("tm", "series"), P("series", None), P("tm", None), P())
    return jax.shard_map(
        on_device,
        mesh=mesh,
        in_specs=placed,
        out_specs=(P("tm", None), P(None, ("series", "tm"))),
        check_vma=False,
    )
```
